32 devices in a mesh: tok: 8 (over z, y), head: 4 (over x, core).
Axes of the slice: x: 2, y: 2, z: 4, core: 2. Of those that a mesh axis runs over, the one named last changes fastest.
Arguments:
- queries: bfloat16 [8192, 4096], P(('tok', 'head')), may hold values from -64 to 64
- keys: bfloat16 [8192, 4096], P(('tok', 'head')), may hold values from -6 to 6
- values: bfloat16 [8192, 4096], P(('tok', 'head')), may hold values from -6 to 6
- token_rates: bfloat16 [8192, 8], P(('tok', 'head')), may hold values from 0.099609375 to 1
- gate_start: bfloat16 [8, 512, 1024], P('head'), may hold values from -0.25 to 0.25
- up_start: bfloat16 [8, 512, 1024], P('head'), may hold values from -0.25 to 0.25
- down_start: bfloat16 [8, 1024, 512], P('head'), may hold values from -0.1875 to 0.1875
- norm_gain: float32 [4096], replicated, may hold values from 0.25 to 1.75
- bounds: int32 [4], replicated, may hold values from 896 to 1152
Outputs:
- layer_out: bfloat16 [8192, 4096], P(('tok', 'head'))
The draws below stay inside these ranges and needn't reach their ends.
Inputs may be any that keep to these rules, and one draw needn't show every extreme that they name: The first span of segment s is its positions below bounds[s].
All inputs are finite; a program needn't handle non-finite values.
Results may differ from the reference program's by a relative error of at most 0.02.
Values may be sent and summed in bfloat16 or wider, within the bound.
A program may use at most 192 MiB of HBM per device.

```python
import math
import jax
import jax.numpy as jnp
from jax import lax

FDIM = 512
HID = 1024
AHD = 128
WINDOW = 512
NS_ITERS = 3
FHEADS = 8
F = 4096
LEN = 2048
TOKENS = 8192
SEQS = 4
BOUND_LO = 896
BOUND_HI = 1152


def paired_fields(key):
    base_q = jnp.clip(jax.random.normal(jax.random.fold_in(key, 11), (TOKENS, F), jnp.float32), -6.0, 6.0)
    base_k = jnp.clip(jax.random.normal(jax.random.fold_in(key, 12), (TOKENS, F), jnp.float32), -6.0, 6.0)
    return (base_q, base_k)


def draw_queries(key, part):
    return paired_fields(key)[0].astype(jnp.bfloat16)


def draw_keys(key, part):
    return paired_fields(key)[1].astype(jnp.bfloat16)


def plant(drawn, own_key, low, top_value):
    longest = drawn.shape.index(max(drawn.shape))
    spots = []
    for shift in (0, 1):
        where = [jax.random.randint(jax.random.fold_in(own_key, axis), (), 0, length) for axis, length in enumerate(drawn.shape)]
        where[longest] = (where[longest] + shift) % drawn.shape[longest]
        spots.append(tuple(where))
    return drawn.at[spots[0]].set(low).at[spots[1]].set(top_value)


def steps_of(key, extent, pieces, least, high):
    def one(position, blocks):
        draws = jax.random.uniform(jax.random.fold_in(jax.random.fold_in(key, 6), position), (blocks,), jnp.float32, least / len(pieces), high / len(pieces))
        return jnp.repeat(jnp.exp(draws), extent[position] // blocks).reshape((-1,) + (1,) * (len(extent) - position - 1))

    level = one(*pieces[0])
    for cut in pieces[1:]:
        level = level * one(*cut)
    return level


def normal_values(own_key, shape, spread, most, split=(), kind=jnp.bfloat16):
    array = jax.random.normal(own_key, shape, jnp.float32) * spread
    if len(split) > 0:
        array = steps_of(own_key, shape, split, -0.22, 0.18) * array
    return jnp.clip(array, min=-most, max=most).astype(kind)


def setup_inputs(seed: int = 0) -> dict:
    seeds = jax.random.split(jax.random.key(seed), 10)
    return {
        "queries": draw_queries(jax.random.fold_in(seeds[9], 71), 0),
        "keys": draw_keys(jax.random.fold_in(seeds[9], 71), 0),
        "values": normal_values(seeds[2], (TOKENS, F), 1.0, 6.0, ((0, 32),)),
        "token_rates": jnp.clip(jnp.exp(math.log(1.0) - 2.306499 * jax.random.uniform(seeds[3], (TOKENS, FHEADS), jnp.float32) ** steps_of(seeds[3], (TOKENS, FHEADS), ((0, 32),), -0.2, 0.2)), 0.099609375, 1.0).astype(jnp.bfloat16),
        "gate_start": normal_values(seeds[4], (FHEADS, FDIM, HID), FDIM ** -0.5, 0.25, ((0, 4),)),
        "up_start": normal_values(seeds[5], (FHEADS, FDIM, HID), FDIM ** -0.5, 0.25, ((0, 4),)),
        "down_start": normal_values(seeds[6], (FHEADS, HID, FDIM), HID ** -0.5, 0.1875, ((0, 4),)),
        "norm_gain": jnp.clip(1.0 + 0.15 * jax.random.normal(seeds[7], (F,), jnp.float32), 0.25, 1.75),
        "bounds": plant(jax.random.randint(seeds[8], (SEQS,), BOUND_LO, BOUND_HI + 1), jax.random.fold_in(seeds[8], 1), BOUND_LO, BOUND_HI).astype(jnp.int32),
    }


linear_coef = 3.4445
cubic_coef = -4.775
quintic_coef = 2.0315
update_step = 1.0
rms_epsilon = 1e-05
norm_epsilon = 1e-06

def silu_slope(pre_act):
    logistic = jax.nn.sigmoid(pre_act)
    return logistic * (1.0 + pre_act * (1.0 - logistic))

def orthogonal(gradient):
    frob_norm = jnp.sqrt(jnp.sum(gradient * gradient) + norm_epsilon)
    iterate = (gradient / frob_norm).astype(jnp.bfloat16)
    for sweep_index in range(NS_ITERS):
        gram_matrix = jnp.dot(iterate, iterate.T, preferred_element_type=jnp.float32).astype(jnp.bfloat16)
        gram_square = jnp.dot(gram_matrix, gram_matrix, preferred_element_type=jnp.float32)
        poly_mix = (cubic_coef * gram_matrix.astype(jnp.float32) + quintic_coef * gram_square).astype(jnp.bfloat16)
        iterate = (linear_coef * iterate.astype(jnp.float32) + jnp.dot(poly_mix, iterate, preferred_element_type=jnp.float32)).astype(jnp.bfloat16)
    return iterate.astype(jnp.float32)

def renorm(updated, w_start):
    start_wide = w_start.astype(jnp.float32)
    target = jnp.sqrt(lax.optimization_barrier(jnp.sum(start_wide * start_wide, axis=0)) + norm_epsilon)
    actual = jnp.sqrt(lax.optimization_barrier(jnp.sum(updated * updated, axis=0)) + norm_epsilon)
    return (updated * (target / actual)).astype(jnp.bfloat16)

def swiglu_apply(in_rows, w_gate, w_up, w_down):
    pre_gate = jnp.dot(in_rows, w_gate, preferred_element_type=jnp.float32)
    pre_up = jnp.dot(in_rows, w_up, preferred_element_type=jnp.float32)
    hidden = (jax.nn.silu(pre_gate) * pre_up).astype(jnp.bfloat16)
    return jnp.dot(hidden, w_down, preferred_element_type=jnp.float32)

def fast_item(q_item, k_item, v_item, rate_row, span_bound, w_gate, w_up, w_down, gain_head):
    length = q_item.shape[0]
    split_low = length // 2 - length // 16
    split_high = length // 2 + length // 16
    in_span = jnp.arange(split_high) < span_bound
    k_rows = k_item[:split_high]
    pre_gate = jnp.dot(k_rows, w_gate, preferred_element_type=jnp.float32)
    pre_up = jnp.dot(k_rows, w_up, preferred_element_type=jnp.float32)
    active = jax.nn.silu(pre_gate)
    hidden = (active * pre_up).astype(jnp.bfloat16)
    weighted = rate_row[:split_high].astype(jnp.float32)[:, None] * v_item[:split_high].astype(jnp.float32)
    target = jnp.where(in_span[:, None], weighted, 0.0).astype(jnp.bfloat16)
    grad_down = jnp.dot(hidden.T, target, preferred_element_type=jnp.float32)
    back_grad = jnp.dot(target, w_down.T, preferred_element_type=jnp.float32)
    d_gate = (back_grad * pre_up * silu_slope(pre_gate)).astype(jnp.bfloat16)
    d_up = (back_grad * active).astype(jnp.bfloat16)
    grad_gate = jnp.dot(k_rows.T, d_gate, preferred_element_type=jnp.float32)
    grad_up = jnp.dot(k_rows.T, d_up, preferred_element_type=jnp.float32)
    new_gate = renorm(w_gate.astype(jnp.float32) + update_step * orthogonal(grad_gate), w_gate)
    new_up = renorm(w_up.astype(jnp.float32) + update_step * orthogonal(grad_up), w_up)
    new_down = renorm(w_down.astype(jnp.float32) + update_step * orthogonal(grad_down.T).T, w_down)
    before_out = swiglu_apply(q_item[:split_high], w_gate, w_up, w_down)
    after_out = swiglu_apply(q_item[split_low:], new_gate, new_up, new_down)
    middle = jnp.where((jnp.arange(split_low, split_high) < span_bound)[:, None], before_out[split_low:], after_out[:split_high - split_low])
    combined = jnp.concatenate([before_out[:split_low], middle, after_out[split_high - split_low:]], axis=0)
    root_mean = jnp.sqrt(lax.optimization_barrier(jnp.mean(combined * combined, axis=-1, keepdims=True)) + rms_epsilon)
    return (combined / root_mean * gain_head.astype(jnp.float32)).astype(jnp.bfloat16)

def attend_stream(queries, keys, values):
    block_len = min(LEN, 512)
    block_count = TOKENS // block_len
    head_count = F // AHD
    padding = jnp.zeros((WINDOW, F), keys.dtype)
    key_padded = jnp.concatenate([padding, keys], axis=0)
    value_padded = jnp.concatenate([padding, values], axis=0)

    def one_block(block_index):
        start = (block_index * block_len).astype(jnp.int32)
        q_rows = lax.dynamic_slice_in_dim(queries, start, block_len, 0)
        k_rows = lax.dynamic_slice_in_dim(key_padded, start, block_len + WINDOW, 0)
        v_rows = lax.dynamic_slice_in_dim(value_padded, start, block_len + WINDOW, 0)
        q_heads = q_rows.astype(jnp.float32).reshape(block_len, head_count, AHD)
        k_heads = k_rows.astype(jnp.float32).reshape(block_len + WINDOW, head_count, AHD)
        v_heads = v_rows.astype(jnp.float32).reshape(block_len + WINDOW, head_count, AHD)
        scores = jnp.einsum('qhd,khd->hqk', q_heads, k_heads) / math.sqrt(AHD)
        query_place = start + jnp.arange(block_len).astype(jnp.int32)
        key_place = start - WINDOW + jnp.arange(block_len + WINDOW).astype(jnp.int32)
        pos_gap = query_place[:, None] - key_place[None, :]
        allowed = ((pos_gap >= 0) & (pos_gap < WINDOW) & (key_place[None, :] >= 0))[None]
        masked = jnp.where(allowed, scores, -jnp.inf)
        row_max = lax.optimization_barrier(jnp.max(masked, axis=-1, keepdims=True))
        weights = jnp.where(allowed, jnp.exp(masked - row_max), 0.0)
        row_total = lax.optimization_barrier(jnp.sum(weights, axis=-1))
        mixed_out = jnp.einsum('hqk,khd->qhd', weights.astype(jnp.bfloat16).astype(jnp.float32), v_heads)
        return (mixed_out / row_total.T[:, :, None]).reshape(block_len, F).astype(jnp.bfloat16)
    return lax.map(one_block, jnp.arange(block_count).astype(jnp.int32)).reshape(TOKENS, F)

def reference(queries, keys, values, token_rates, gate_start, up_start, down_start, norm_gain, bounds):
    attn = attend_stream(queries, keys, values)

    def split_heads(block):
        return block.reshape(SEQS, LEN, FHEADS, FDIM).transpose(0, 2, 1, 3)
    rate_items = token_rates.reshape(SEQS, LEN, FHEADS).transpose(0, 2, 1)
    gain_items = norm_gain.reshape(FHEADS, FDIM)

    def per_sequence(seq_args):
        span_bound = seq_args[4]

        def per_head(head_args):
            return fast_item(head_args[0], head_args[1], head_args[2], head_args[3], span_bound, head_args[4], head_args[5], head_args[6], head_args[7])
        return lax.map(per_head, (seq_args[0], seq_args[1], seq_args[2], seq_args[3], gate_start, up_start, down_start, gain_items))
    fast_items = lax.map(per_sequence, (split_heads(queries), split_heads(keys), split_heads(values), rate_items, bounds))
    fast_rows = fast_items.transpose(0, 2, 1, 3).reshape(TOKENS, F)
    return (attn.astype(jnp.float32) + fast_rows.astype(jnp.float32)).astype(jnp.bfloat16)
```

```python
import functools
import math
from types import SimpleNamespace

import jax
import jax.numpy as jnp
from jax import lax
from jax.experimental import pallas as pl
from jax.experimental.pallas import tpu as pltpu
from jax.sharding import PartitionSpec as P

AHD = 128
WINDOW = 512
NS_ITERS = 3
CHUNK = 512

linear_coef = 3.4445
cubic_coef = -4.775
quintic_coef = 2.0315
rms_epsilon = 1e-05
norm_epsilon = 1e-06
MESH = pl.DeviceIdType.MESH
F32 = jnp.float32
BF16 = jnp.bfloat16


def mm(a, b, ca=1, cb=0):
    return lax.dot_general(a, b, (((ca,), (cb,)), ((), ())), preferred_element_type=F32)


def logistic(x):
    return 0.5 * jnp.tanh(0.5 * x) + 0.5


def loop(count, fn):
    def step(i, carry):
        fn(i)
        return carry

    lax.fori_loop(0, count, step, 0)


def at(start, size, multiple):
    return pl.ds(pl.multiple_of(start, multiple), size)


def transpose_down(c):
    def step(i):
        cols = at(i * CHUNK, CHUNK, CHUNK)
        c.wdt[:, cols] = c.wd[cols, :].T

    loop(c.hid_width // CHUNK, step)


def clear_gradients(c):
    def step(i):
        c.grad[:, at(i * 64, 64, 64), :] = jnp.zeros((3, 64, c.hid_width), F32)

    loop(c.width // 64, step)


def train_rows(c, block, start, size):
    for i in range(size // 128):
        part = slice(i * 128, (i + 1) * 128)
        here = at(WINDOW + start + i * 128, 128, 128)
        rates = c.rates[block, :, part].astype(F32)
        mine = lax.broadcasted_iota(jnp.int32, rates.shape, 0) == c.feature
        rates = jnp.sum(jnp.where(mine, rates, 0.0), axis=0, keepdims=True)
        rate_col = jnp.broadcast_to(rates, (128, 128)).T[:, 0:1]
        place = start + i * 128 + lax.broadcasted_iota(jnp.int32, (128, c.width), 0)
        target = jnp.where(place < c.bound, rate_col * c.v[here, :].astype(F32), 0.0)
        c.target[part, :] = target.astype(BF16)
        c.target_t[:, part] = target.T.astype(BF16)
        c.k_t[:, part] = c.k[here, :].T
    k_rows = c.k[at(WINDOW + start, size, 128), :]
    for i in range(c.hid_width // CHUNK):
        cols = slice(i * CHUNK, (i + 1) * CHUNK)
        gate = mm(k_rows, c.wg[:, cols])
        up = mm(k_rows, c.wu[:, cols])
        sig = logistic(gate)
        act = gate * sig
        slope = up * (sig + act * (1.0 - sig))
        back = mm(c.target[:size, :], c.wdt[:, cols])
        lefts = (c.k_t, c.k_t, c.target_t)
        rights = (back * slope, back * act, act * up)
        for m, (left, right) in enumerate(zip(lefts, rights)):
            c.grad[m, :, cols] += mm(left[:, :size], right.astype(BF16))


def scale_gradients(c):
    def scale(m):
        grad = c.grad[m]
        frob = lax.rsqrt(jnp.sum(grad * grad, keepdims=True) + norm_epsilon)
        c.x[0, m] = (grad * frob).astype(BF16)

    loop(3, scale)


def sweep(c, turn):
    old, new = turn % 2, (turn + 1) % 2
    for m in range(3):
        x = c.x[old, m]
        c.a[m] = mm(x, x, 1, 1).astype(BF16)
    for m in range(3):
        a = c.a[m]
        c.p[m] = (cubic_coef * a.astype(F32) + quintic_coef * mm(a, a)).astype(BF16)
    for m in range(3):
        x = c.x[old, m]
        c.x[new, m] = (linear_coef * x.astype(F32) + mm(c.p[m], x)).astype(BF16)


def renorm(c):
    def by_column(i):
        cols = at(i * CHUNK, CHUNK, CHUNK)
        for m, ref in ((0, c.wg), (1, c.wu)):
            w = ref[:, cols].astype(F32)
            u = w + c.x[NS_ITERS % 2, m, :, cols].astype(F32)
            want = jnp.sqrt(jnp.sum(w * w, axis=0, keepdims=True) + norm_epsilon)
            have = jnp.sqrt(jnp.sum(u * u, axis=0, keepdims=True) + norm_epsilon)
            c.x[NS_ITERS % 2, m, :, cols] = (u * (want / have)).astype(BF16)

    loop(c.hid_width // CHUNK, by_column)

    def by_row(i):
        rows = at(i * 128, 128, 128)
        w = c.wdt[rows, :].astype(F32)
        u = w + c.x[NS_ITERS % 2, 2, rows, :].astype(F32)
        want = jnp.sqrt(jnp.sum(w * w, axis=1, keepdims=True) + norm_epsilon)
        have = jnp.sqrt(jnp.sum(u * u, axis=1, keepdims=True) + norm_epsilon)
        c.x[NS_ITERS % 2, 2, rows, :] = (u * (want / have)).astype(BF16)

    loop(c.width // 128, by_row)


def attention(c, first, count):
    tile = WINDOW // 2
    power = math.log2(math.e) / math.sqrt(AHD)

    def step(i):
        t = first + i
        rows = at(t * tile, tile, tile)
        span = at(t * tile, WINDOW + tile, tile)
        below = lax.broadcasted_iota(jnp.int32, (tile, tile), 1) <= lax.broadcasted_iota(
            jnp.int32, (tile, tile), 0
        )
        far_bias = jnp.where(c.first_segment * (2 - t) > 0, F32(-1e30), F32(0.0))
        mid_bias = jnp.where(c.first_segment * (1 - t) > 0, F32(-1e30), F32(0.0))
        for head in range(c.width // AHD):
            feats = slice(head * AHD, (head + 1) * AHD)
            scores = mm(c.q[rows, feats], c.k[span, feats], 1, 1)
            edge = jnp.where(below, scores[:, 2 * tile :], scores[:, :tile] + far_bias)
            mid = scores[:, tile : 2 * tile] + mid_bias
            top = jnp.max(jnp.maximum(edge, mid), axis=1, keepdims=True)
            edge = jnp.exp2((edge - top) * power)
            mid = jnp.exp2((mid - top) * power)
            total = jnp.sum(edge + mid, axis=1, keepdims=True)
            weights = jnp.concatenate(
                [
                    jnp.where(below, 0.0, edge).astype(BF16),
                    mid.astype(BF16),
                    jnp.where(below, edge, 0.0).astype(BF16),
                ],
                axis=1,
            )
            mixed = mm(weights, c.v[span, feats])
            c.out[rows, feats] = (mixed / total).astype(BF16)

    loop(count, step)


def swiglu(c, start, size, gate, up, down, down_dim):
    q_rows = c.q[at(start, size, 128), :]
    for i in range(c.hid_width // CHUNK):
        cols = slice(i * CHUNK, (i + 1) * CHUNK)
        pre_gate = mm(q_rows, gate[:, cols])
        pre_up = mm(q_rows, up[:, cols])
        c.apply_hid[:size, cols] = (pre_gate * logistic(pre_gate) * pre_up).astype(BF16)
    return mm(c.apply_hid[:size, :], down[...], 1, down_dim)


def old_rows(c, start, size):
    return swiglu(c, start, size, c.wg, c.wu, c.wd, 0)


def new_rows(c, start, size):
    new = c.x.at[NS_ITERS % 2]
    return swiglu(c, start, size, new.at[0], new.at[1], new.at[2], 1)


def finish_rows(c, start, raw):
    rows = at(start, raw.shape[0], 128)
    scale = lax.rsqrt(jnp.mean(raw * raw, axis=1, keepdims=True) + rms_epsilon)
    fast = (raw * scale * c.gain[c.feature]).astype(BF16)
    c.out[rows, :] = (c.out[rows, :].astype(F32) + fast.astype(F32)).astype(BF16)


def below_bound(c, start, shape):
    return start + lax.broadcasted_iota(jnp.int32, shape, 0) < c.bound


def fast_old(c, quarter):
    size, edge = c.quarter, c.high - c.low
    edge //= 2
    start = quarter * size
    c.raw[...] = old_rows(c, start, size)
    finish_rows(c, start, c.raw[: size - edge, :])

    @pl.when(quarter == 0)
    def _():
        finish_rows(c, start + size - edge, c.raw[size - edge :, :])

    @pl.when(quarter == 1)
    def _():
        c.open_raw[...] = c.raw[size - edge :, :]


def close_edge(c):
    edge = (c.high - c.low) // 2
    after = new_rows(c, c.low, edge)
    finish_rows(c, c.low, jnp.where(below_bound(c, c.low, after.shape), c.open_raw[...], after))


def fast_new(c, quarter):
    size, edge = c.quarter, (c.high - c.low) // 2
    start = quarter * size
    c.raw[...] = new_rows(c, start, size)

    @pl.when(quarter == 2)
    def _():
        before = old_rows(c, start, edge)
        after = c.raw[:edge, :]
        c.raw[:edge, :] = jnp.where(below_bound(c, start, after.shape), before, after)

    finish_rows(c, start, c.raw[...])


def scratch_of(length, width, hid_width, rows, peers):
    dma = pltpu.SemaphoreType.DMA
    quarter, edge = length // 4, length // 16
    return {
        "q": pltpu.VMEM((length, width), BF16),
        "k": pltpu.VMEM((WINDOW + length, width), BF16),
        "v": pltpu.VMEM((WINDOW + length, width), BF16),
        "my_rates": pltpu.VMEM((peers, rows), BF16),
        "rates": pltpu.VMEM((peers, peers, rows), BF16),
        "gain": pltpu.VMEM((peers, 1, width), F32),
        "out": pltpu.VMEM((length, width), BF16),
        "kv_send": dma((2, 2, peers)),
        "kv_recv": dma((2, 2, peers)),
        "q_send": dma((peers,)),
        "q_recv": dma((peers,)),
        "rate_send": dma((peers,)),
        "rate_recv": dma((peers,)),
        "own_sem": dma((3,)),
        "halo_send": dma((2,)),
        "halo_recv": dma((2,)),
        "out_send": dma((peers,)),
        "out_recv": dma((peers,)),
        "out_own": dma,
        "wg": pltpu.VMEM((width, hid_width), BF16),
        "wu": pltpu.VMEM((width, hid_width), BF16),
        "wd": pltpu.VMEM((hid_width, width), BF16),
        "wdt": pltpu.VMEM((width, hid_width), BF16),
        "target": pltpu.VMEM((rows, width), BF16),
        "target_t": pltpu.VMEM((width, rows), BF16),
        "k_t": pltpu.VMEM((width, rows), BF16),
        "grad": pltpu.VMEM((3, width, hid_width), F32),
        "x": pltpu.VMEM((2, 3, width, hid_width), BF16),
        "a": pltpu.VMEM((3, width, width), BF16),
        "p": pltpu.VMEM((3, width, width), BF16),
        "apply_hid": pltpu.VMEM((quarter, hid_width), BF16),
        "raw": pltpu.VMEM((quarter, width), F32),
        "open_raw": pltpu.VMEM((edge, width), F32),
        "w_sem": dma((5,)),
    }


def sizes(length, width, hid_width, rows):
    low, high = length // 2 - length // 16, length // 2 + length // 16
    return dict(
        length=length, width=width, hid_width=hid_width, rows=rows, low=low, high=high, quarter=length // 4
    )


def flip(index, distance, count):
    result, place = 0, 1
    while place < count:
        bit = (index // place) % 2
        result = result + place * (1 - bit if distance & place else bit)
        place *= 2
    return result


def flip_by(index, distance, count):
    result, place = 0, 1
    while place < count:
        bit, other = (index // place) % 2, (distance // place) % 2
        result = result + place * (bit + other - 2 * bit * other)
        place *= 2
    return result


def place_of(peer, tok, group):
    return (tok - tok % 2 + peer // group, peer % group)


def feature_of(peer, group):
    return 2 * (peer % group) + peer // group


def greet(others, neighbours, meanwhile):
    barrier = pltpu.get_barrier_semaphore()
    count = len(others)
    for other in others:
        pl.semaphore_signal(barrier, inc=1, device_id=other, device_id_type=MESH)
    for exists, other in neighbours:
        count = count + jnp.where(exists, 1, 0)

        @pl.when(exists)
        def _(other=other):
            pl.semaphore_signal(barrier, inc=1, device_id=other, device_id_type=MESH)

    meanwhile()
    pl.semaphore_wait(barrier, count)


def pick(index, values):
    result = values[-1]
    for i, value in enumerate(values[:-1]):
        result = jnp.where(index == i, value, result)
    return result


def kernel(
    names, dims, group, toks, bounds, gain, q, k, v, r, gate_all, up_all, down_all, out, *scratch
):
    c = SimpleNamespace(**dims, **dict(zip(names, scratch)))
    tok, column = lax.axis_index("tok"), lax.axis_index("head")
    parity = tok % 2
    peers, rows, width = 2 * group, c.rows, c.width
    half, part = group // 2, rows // 2
    side = column // half
    me = parity * group + column
    first_late = group
    after = ((tok + 2) % toks, column)
    before = ((tok + toks - 2) % toks, column)
    has_after, has_before = tok < toks - 2, tok >= 2
    c.feature = 2 * column + parity
    c.bound = bounds[tok // 2]
    c.first_segment = jnp.where(tok < 2, 1, 0)
    loads = [
        pltpu.make_async_copy(source, mine, c.w_sem.at[i])
        for i, (source, mine) in enumerate(
            (
                (r, c.my_rates),
                (gain, c.gain),
                (gate_all.at[parity], c.wg),
                (up_all.at[parity], c.wu),
                (down_all.at[parity], c.wd),
            )
        )
    ]

    def columns(peer):
        return at(feature_of(peer, group) * width, width, width)

    def slot(t, start, size):
        return (c.k, c.v, c.q)[t].at[at((WINDOW if t < 2 else 0) + start, size, 128), :]

    owns = [
        pltpu.make_async_copy((k, v, q)[t].at[:, columns(me)], slot(t, me * rows, rows), c.own_sem.at[t])
        for t in range(3)
    ]

    def load():
        for copy in loads + owns:
            copy.start()
        loads[0].wait()
        c.rates[me] = c.my_rates[...]

    everybody = [place_of(flip(me, d, peers), tok, group) for d in range(1, peers)]
    greet(everybody, ((has_after, after), (has_before, before)), load)

    def remote(source, target, send, recv, peer):
        return pltpu.make_async_remote_copy(
            source, target, send, recv, device_id=place_of(peer, tok, group), device_id_type=MESH
        )

    def kv_copy(t, h, peer):
        return remote(
            (k, v)[t].at[pl.ds(h * part, part), columns(peer)],
            slot(t, me * rows + h * part, part),
            c.kv_send.at[t, h, peer], c.kv_recv.at[t, h, me], peer,
        )

    def q_copy(peer):
        return remote(
            q.at[:, columns(peer)], slot(2, me * rows, rows), c.q_send.at[peer], c.q_recv.at[me], peer
        )

    def rate_copy(peer):
        return remote(c.my_rates, c.rates.at[me], c.rate_send.at[peer], c.rate_recv.at[me], peer)

    def got_kv(peer, h):
        @pl.when(me != peer)
        def _():
            for t in range(2):
                target = slot(t, peer * rows + h * part, part)
                remote(target, target, c.kv_send.at[t, h, peer], c.kv_recv.at[t, h, peer], peer).wait_recv()

    def got_q(peer):
        @pl.when(me != peer)
        def _():
            target = slot(2, peer * rows, rows)
            remote(target, target, c.q_send.at[peer], c.q_recv.at[peer], peer).wait_recv()

    def got_rates(peer):
        @pl.when(me != peer)
        def _():
            target = c.rates.at[peer]
            remote(target, target, c.rate_send.at[peer], c.rate_recv.at[peer], peer).wait_recv()

    def block(peer):
        return out.at[:, columns(peer)]

    def done_rows(peer):
        return c.out.at[at(peer * rows, rows, rows), :]

    def give(peer):
        return remote(done_rows(peer), block(me), c.out_send.at[peer], c.out_recv.at[me], peer)

    def taken(peer):
        return remote(done_rows(peer), block(peer), c.out_send.at[peer], c.out_recv.at[peer], peer)

    keep = pltpu.make_async_copy(done_rows(me), block(me), c.out_own)

    def hand_out(peer):
        @pl.when(peer != me)
        def _():
            give(peer).start()

        @pl.when(peer == me)
        def _():
            keep.start()

    halos = [
        pltpu.make_async_remote_copy(
            o.at[pl.ds(c.length, WINDOW), :], o.at[pl.ds(0, WINDOW), :],
            c.halo_send.at[t], c.halo_recv.at[t], device_id=after, device_id_type=MESH,
        )
        for t, o in enumerate((c.k, c.v))
    ]

    chip = list(range(1, half))
    along = list(range(half, group))
    across = list(range(group, group + half))
    corner = list(range(group + half, peers))
    near = [d for pair in zip(along, across) for d in pair]
    everyone = chip + near + corner

    def send_kv(ds, hs=(0, 1), owner=True):
        for d in ds:
            for h in hs:
                def start():
                    for t in range(2):
                        kv_copy(t, h, flip(me, d, peers)).start()

                if h == 0 and owner:
                    pl.when(me != first_late)(start)
                else:
                    start()

    def send_q(ds):
        for d in ds:
            q_copy(flip(me, d, peers)).start()

    has_rates = (parity == 0) | (me == first_late)

    @pl.when(has_rates)
    def _():
        for d in everyone:
            rate_copy(flip(me, d, peers)).start()

    @pl.when(me == first_late)
    def _():
        send_kv(corner + near + chip, (0,), False)

    send_kv(chip + near)
    send_q(chip)

    @pl.when(parity == 1)
    def _():
        send_q(near)

    def send_corner():
        send_kv(corner)
        send_q(corner)

    pl.when((parity == 0) | (side == 0))(send_corner)

    @pl.when(parity == 0)
    def _():
        send_q(along)

    for copy in loads[1:] + owns:
        copy.wait()
    transpose_down(c)
    clear_gradients(c)

    @pl.when(tok < 2)
    def _():
        c.k[:WINDOW, :] = jnp.zeros((WINDOW, width), BF16)
        c.v[:WINDOW, :] = jnp.zeros((WINDOW, width), BF16)

    tiles = c.quarter // (WINDOW // 2)

    def got_first_late():
        got_kv(first_late, 1)
        for p in range(group + 1, group + half):
            for h in range(2):
                got_kv(p, h)

    def got_last():
        for p in range(group + half, peers):
            for h in range(2):
                got_kv(p, h)
        for halo in halos:
            pl.when(has_after)(halo.start)

    def attend(quarter):
        for j in range(half):
            got_q(quarter * half + j)

        @pl.when(quarter == 0)
        def _():
            for halo in halos:
                pl.when(has_before)(halo.wait_recv)

        attention(c, quarter * tiles, tiles)

    def train(i):
        p = flip_by(column, i, group)
        got_rates(p)
        for h in range(2):
            got_kv(p, h)
        train_rows(c, p, p * rows, rows)

        @pl.when(i == half - 1)
        def _():
            got_rates(first_late)
            got_kv(first_late, 0)
            train_rows(c, first_late, c.length // 2, part)

            @pl.when(parity == 1)
            def _():
                got_first_late()
                got_last()
                attend(3)

                @pl.when(side == 1)
                def _():
                    got_q(2 * half)
                    send_corner()
                    got_q(2 * half + 1)
                    attention(c, 2 * tiles, tiles)

    loop(group, train)

    @pl.when((parity == 0) & (side == 0))
    def _():
        got_first_late()

    @pl.when((parity == 0) & (side == 1))
    def _():
        got_last()

    scale_gradients(c)

    def improve(i):
        sweep(c, i)
        quarter = 1 - side

        @pl.when((parity == 1) & (i == 0))
        def _():
            attend(quarter)
            fast_old(c, quarter)
            for j in range(half):
                pl.when((quarter == 0) | (j < half - 1))(
                    functools.partial(hand_out, quarter * half + j)
                )

    loop(NS_ITERS, improve)
    renorm(c)

    def last(s):
        early = jnp.where(side == 0, pick(s, (2, 1, 3, 0)), pick(s, (1, 3, 0, 2)))
        late = pick(s, (3 - side, side, 2 + side))
        quarter = jnp.where(parity == 0, early, late)

        @pl.when((parity == 0) & (s == 1))
        def _():
            pl.when(side == 0)(got_last)
            pl.when(side == 1)(got_first_late)

        @pl.when((parity == 0) | (s == 1) | ((s == 2) & (side == 0)))
        def _():
            attend(quarter)

        @pl.when(quarter < 2)
        def _():
            fast_old(c, quarter)

        @pl.when(quarter >= 2)
        def _():
            fast_new(c, quarter)

        for j in range(half):
            pl.when((quarter != 1) | (j < half - 1))(
                functools.partial(hand_out, quarter * half + j)
            )

        @pl.when((quarter == 1) | ((parity == 1) & (side == 0) & (s == 0)))
        def _():
            close_edge(c)
            hand_out(group - 1)

        @pl.when((parity == 0) & (s == 0))
        def _():
            send_q(across)

    loop(jnp.where(parity == 0, 4, 3), last)
    keep.wait()
    for d in everyone:
        taken(flip(me, d, peers)).wait_recv()
    for d in everyone:
        peer = flip(me, d, peers)
        give(peer).wait_send()
        q_copy(peer).wait_send()
        for t in range(2):
            for h in range(2):
                kv_copy(t, h, peer).wait_send()
    for halo in halos:
        pl.when(has_after)(halo.wait_send)

    @pl.when(has_rates)
    def _():
        for d in everyone:
            rate_copy(flip(me, d, peers)).wait_send()


def body(queries, keys, values, token_rates, gate_start, up_start, down_start, norm_gain, bounds):
    rows, feats = queries.shape
    group, toks = lax.axis_size("head"), lax.axis_size("tok")
    heads, width, hid_width = token_rates.shape[1], gate_start.shape[1], gate_start.shape[2]
    peers = 2 * group
    length = peers * rows
    anywhere = pl.BlockSpec(memory_space=pl.ANY)
    scratch = scratch_of(length, width, hid_width, rows, peers)
    return pl.pallas_call(
        functools.partial(
            kernel, tuple(scratch), sizes(length, width, hid_width, rows), group, toks
        ),
        out_shape=jax.ShapeDtypeStruct((rows, feats), BF16),
        in_specs=[pl.BlockSpec(memory_space=pltpu.SMEM)] + [anywhere] * 8,
        out_specs=anywhere,
        scratch_shapes=list(scratch.values()),
        compiler_params=pltpu.CompilerParams(
            collective_id=0, has_side_effects=True, vmem_limit_bytes=66000000
        ),
        name="layer",
    )(
        bounds, norm_gain.reshape(heads, 1, width), queries, keys, values, token_rates.T,
        gate_start, up_start, down_start,
    )


def solution(mesh):
    spread = P(("tok", "head"), None)
    owned = P("head", None, None)
    return jax.shard_map(
        body,
        mesh=mesh,
        in_specs=(spread,) * 4 + (owned,) * 3 + (P(), P()),
        out_specs=spread,
        check_vma=False,
    )
```

```python
import functools
import math
from types import SimpleNamespace

import jax
import jax.numpy as jnp
from jax import lax
from jax.experimental import pallas as pl
from jax.experimental.pallas import tpu as pltpu
from jax.sharding import PartitionSpec as P

AHD = 128
WINDOW = 512
NS_ITERS = 3
CHUNK = 512

linear_coef = 3.4445
cubic_coef = -4.775
quintic_coef = 2.0315
rms_epsilon = 1e-05
norm_epsilon = 1e-06
MESH = pl.DeviceIdType.MESH
F32 = jnp.float32
BF16 = jnp.bfloat16


def mm(a, b, ca=1, cb=0):
    return lax.dot_general(a, b, (((ca,), (cb,)), ((), ())), preferred_element_type=F32)


def logistic(x):
    return 0.5 * jnp.tanh(0.5 * x) + 0.5


def loop(count, fn):
    def step(i, carry):
        fn(i)
        return carry

    lax.fori_loop(0, count, step, 0)


def at(start, size, multiple):
    return pl.ds(pl.multiple_of(start, multiple), size)


def transpose_down(c):
    def step(i):
        cols = at(i * CHUNK, CHUNK, CHUNK)
        c.wdt[:, cols] = c.wd[cols, :].T

    loop(c.hid_width // CHUNK, step)


def clear_gradients(c):
    def step(i):
        c.grad[:, at(i * 64, 64, 64), :] = jnp.zeros((3, 64, c.hid_width), F32)

    loop(c.width // 64, step)


def train_rows(c, block, start, size):
    for i in range(size // 128):
        part = slice(i * 128, (i + 1) * 128)
        here = at(WINDOW + start + i * 128, 128, 128)
        rates = c.rates[block, :, part].astype(F32)
        mine = lax.broadcasted_iota(jnp.int32, rates.shape, 0) == c.feature
        rates = jnp.sum(jnp.where(mine, rates, 0.0), axis=0, keepdims=True)
        rate_col = jnp.broadcast_to(rates, (128, 128)).T[:, 0:1]
        place = start + i * 128 + lax.broadcasted_iota(jnp.int32, (128, c.width), 0)
        target = jnp.where(place < c.bound, rate_col * c.v[here, :].astype(F32), 0.0)
        c.target[part, :] = target.astype(BF16)
        c.target_t[:, part] = target.T.astype(BF16)
        c.k_t[:, part] = c.k[here, :].T
    k_rows = c.k[at(WINDOW + start, size, 128), :]
    for i in range(c.hid_width // CHUNK):
        cols = slice(i * CHUNK, (i + 1) * CHUNK)
        gate = mm(k_rows, c.wg[:, cols])
        up = mm(k_rows, c.wu[:, cols])
        sig = logistic(gate)
        act = gate * sig
        slope = up * (sig + act * (1.0 - sig))
        back = mm(c.target[:size, :], c.wdt[:, cols])
        lefts = (c.k_t, c.k_t, c.target_t)
        rights = (back * slope, back * act, act * up)
        for m, (left, right) in enumerate(zip(lefts, rights)):
            total = c.grad[m, :, cols] + mm(left[:, :size], right.astype(BF16))
            c.grad[m, :, cols] = total
            c.squares[m, :, cols] = jnp.sum((total * total).reshape(-1, 8, CHUNK), axis=0)


def scale_gradients(c):
    for m in range(3):
        frob = lax.rsqrt(jnp.sum(c.squares[m], keepdims=True) + norm_epsilon)
        c.x[0, m] = (c.grad[m] * frob).astype(BF16)


def symmetric(ref, m, size, top, corner):
    ref[m, :size, :] = top
    ref[m, size:, size:] = corner
    ref[m, size:, :size] = top[:, size:].T


def sweep(c, turn):
    old, new, h = turn % 2, (turn + 1) % 2, c.width // 2
    for m in range(3):
        x = c.x[old, m]
        top, corner = mm(x[:h], x, 1, 1), mm(x[h:], x[h:], 1, 1)
        symmetric(c.a, m, h, top.astype(BF16), corner.astype(BF16))
    for m in range(3):
        a = c.a[m]
        top = cubic_coef * a[:h].astype(F32) + quintic_coef * mm(a[:h], a)
        corner = cubic_coef * a[h:, h:].astype(F32) + quintic_coef * mm(a[h:], a[:, h:])
        symmetric(c.p, m, h, top.astype(BF16), corner.astype(BF16))
    for m in range(3):
        x = c.x[old, m]
        c.x[new, m] = (linear_coef * x.astype(F32) + mm(c.p[m], x)).astype(BF16)


def measure_start(c):
    for m, ref in ((0, c.wg), (1, c.wu)):
        for i in range(c.hid_width // CHUNK):
            cols = slice(i * CHUNK, (i + 1) * CHUNK)
            w = ref[:, cols].astype(F32)
            c.want[m, :, cols] = jnp.sqrt(jnp.sum(w * w, axis=0, keepdims=True) + norm_epsilon)

    def by_row(i):
        rows = at(i * 128, 128, 128)
        w = c.wdt[rows, :].astype(F32)
        c.want_down[rows, :] = jnp.sqrt(jnp.sum(w * w, axis=1, keepdims=True) + norm_epsilon)

    loop(c.width // 128, by_row)


def renorm(c):
    x = c.x.at[NS_ITERS % 2]
    for m, ref in ((0, c.wg), (1, c.wu)):
        for i in range(c.hid_width // CHUNK):
            cols = slice(i * CHUNK, (i + 1) * CHUNK)
            u = ref[:, cols].astype(F32) + x[m, :, cols].astype(F32)
            have = lax.rsqrt(jnp.sum(u * u, axis=0, keepdims=True) + norm_epsilon)
            x[m, :, cols] = (u * (c.want[m, :, cols] * have)).astype(BF16)
    for i in range(c.width // 128):
        rows = slice(i * 128, (i + 1) * 128)
        u = c.wdt[rows, :].astype(F32) + x[2, rows, :].astype(F32)
        have = lax.rsqrt(jnp.sum(u * u, axis=1, keepdims=True) + norm_epsilon)
        x[2, rows, :] = (u * (c.want_down[rows, :] * have)).astype(BF16)


def attention(c, first, count):
    tile = WINDOW // 2
    power = math.log2(math.e) / math.sqrt(AHD)

    def step(i):
        t = first + i
        rows = at(t * tile, tile, tile)
        span = at(t * tile, WINDOW + tile, tile)
        below = lax.broadcasted_iota(jnp.int32, (tile, tile), 1) <= lax.broadcasted_iota(
            jnp.int32, (tile, tile), 0
        )
        far_bias = jnp.where(c.first_segment * (2 - t) > 0, F32(-1e30), F32(0.0))
        mid_bias = jnp.where(c.first_segment * (1 - t) > 0, F32(-1e30), F32(0.0))
        for head in range(c.width // AHD):
            feats = slice(head * AHD, (head + 1) * AHD)
            scores = mm(c.q[rows, feats], c.k[span, feats], 1, 1)
            edge = jnp.where(below, scores[:, 2 * tile :], scores[:, :tile] + far_bias)
            mid = scores[:, tile : 2 * tile] + mid_bias
            top = jnp.max(jnp.maximum(edge, mid), axis=1, keepdims=True)
            edge = jnp.exp2((edge - top) * power)
            mid = jnp.exp2((mid - top) * power)
            total = jnp.sum(edge + mid, axis=1, keepdims=True)
            weights = jnp.concatenate(
                [
                    jnp.where(below, 0.0, edge).astype(BF16),
                    mid.astype(BF16),
                    jnp.where(below, edge, 0.0).astype(BF16),
                ],
                axis=1,
            )
            mixed = mm(weights, c.v[span, feats])
            c.out[rows, feats] = (mixed / total).astype(BF16)

    loop(count, step)


def swiglu(c, start, size, gate, up, down, down_dim):
    q_rows = c.q[at(start, size, 128), :]
    for i in range(c.hid_width // CHUNK):
        cols = slice(i * CHUNK, (i + 1) * CHUNK)
        pre_gate = mm(q_rows, gate[:, cols])
        pre_up = mm(q_rows, up[:, cols])
        c.apply_hid[:size, cols] = (pre_gate * logistic(pre_gate) * pre_up).astype(BF16)
    return mm(c.apply_hid[:size, :], down[...], 1, down_dim)


def old_rows(c, start, size):
    return swiglu(c, start, size, c.wg, c.wu, c.wd, 0)


def new_rows(c, start, size):
    new = c.x.at[NS_ITERS % 2]
    return swiglu(c, start, size, new.at[0], new.at[1], new.at[2], 1)


def finish_rows(c, start, raw):
    rows = at(start, raw.shape[0], 128)
    scale = lax.rsqrt(jnp.mean(raw * raw, axis=1, keepdims=True) + rms_epsilon)
    fast = (raw * scale * c.gain[c.feature]).astype(BF16)
    c.out[rows, :] = (c.out[rows, :].astype(F32) + fast.astype(F32)).astype(BF16)


def below_bound(c, start, shape):
    return start + lax.broadcasted_iota(jnp.int32, shape, 0) < c.bound


def fast_old(c, block):
    size = c.rows // 2
    start = block * c.rows
    c.raw[...] = old_rows(c, start, c.rows)
    finish_rows(c, start, c.raw[:size, :])

    @pl.when(start + c.rows <= c.low)
    def _():
        finish_rows(c, start + size, c.raw[size:, :])

    @pl.when(start + c.rows > c.low)
    def _():
        c.open_raw[...] = c.raw[size:, :]


def close_edge(c):
    after = new_rows(c, c.low, c.rows // 2)
    finish_rows(c, c.low, jnp.where(below_bound(c, c.low, after.shape), c.open_raw[...], after))


def fast_new(c, block):
    size = c.rows // 2
    start = block * c.rows
    c.raw[...] = new_rows(c, start, c.rows)

    @pl.when(start < c.high)
    def _():
        before = old_rows(c, start, size)
        after = c.raw[:size, :]
        c.raw[:size, :] = jnp.where(below_bound(c, start, after.shape), before, after)

    finish_rows(c, start, c.raw[...])


def scratch_of(length, width, hid_width, rows, peers):
    dma = pltpu.SemaphoreType.DMA
    return {
        "q": pltpu.VMEM((length, width), BF16),
        "k": pltpu.VMEM((WINDOW + length, width), BF16),
        "v": pltpu.VMEM((WINDOW + length, width), BF16),
        "my_rates": pltpu.VMEM((peers, rows), BF16),
        "rates": pltpu.VMEM((peers, peers, rows), BF16),
        "gain": pltpu.VMEM((peers, 1, width), F32),
        "out": pltpu.VMEM((length, width), BF16),
        "kv_send": dma((2, 2, peers)),
        "kv_recv": dma((2, 2, peers)),
        "q_send": dma((peers,)),
        "q_recv": dma((peers,)),
        "rate_send": dma((peers,)),
        "rate_recv": dma((peers,)),
        "own_sem": dma((3,)),
        "halo_send": dma((2,)),
        "halo_recv": dma((2,)),
        "out_send": dma((peers,)),
        "out_recv": dma((peers,)),
        "out_own": dma,
        "wg": pltpu.VMEM((width, hid_width), BF16),
        "wu": pltpu.VMEM((width, hid_width), BF16),
        "wd": pltpu.VMEM((hid_width, width), BF16),
        "wdt": pltpu.VMEM((width, hid_width), BF16),
        "target": pltpu.VMEM((rows, width), BF16),
        "target_t": pltpu.VMEM((width, rows), BF16),
        "k_t": pltpu.VMEM((width, rows), BF16),
        "grad": pltpu.VMEM((3, width, hid_width), F32),
        "squares": pltpu.VMEM((3, 8, hid_width), F32),
        "want": pltpu.VMEM((2, 1, hid_width), F32),
        "want_down": pltpu.VMEM((width, 1), F32),
        "x": pltpu.VMEM((2, 3, width, hid_width), BF16),
        "a": pltpu.VMEM((3, width, width), BF16),
        "p": pltpu.VMEM((3, width, width), BF16),
        "apply_hid": pltpu.VMEM((rows, hid_width), BF16),
        "raw": pltpu.VMEM((rows, width), F32),
        "open_raw": pltpu.VMEM((rows // 2, width), F32),
        "w_sem": dma((5,)),
    }


def sizes(length, width, hid_width, rows):
    low, high = length // 2 - length // 16, length // 2 + length // 16
    return dict(
        length=length, width=width, hid_width=hid_width, rows=rows, low=low, high=high
    )


def flip(index, distance, count):
    result, place = 0, 1
    while place < count:
        bit = (index // place) % 2
        result = result + place * (1 - bit if distance & place else bit)
        place *= 2
    return result


def flip_by(index, distance, count):
    result, place = 0, 1
    while place < count:
        bit, other = (index // place) % 2, (distance // place) % 2
        result = result + place * (bit + other - 2 * bit * other)
        place *= 2
    return result


def place_of(peer, tok, group):
    return (tok - tok % 2 + peer // group, peer % group)


def feature_of(peer, group):
    return 2 * (peer % group) + peer // group


def greet(others, neighbours, meanwhile):
    barrier = pltpu.get_barrier_semaphore()
    count = len(others)
    for other in others:
        pl.semaphore_signal(barrier, inc=1, device_id=other, device_id_type=MESH)
    for exists, other in neighbours:
        count = count + jnp.where(exists, 1, 0)

        @pl.when(exists)
        def _(other=other):
            pl.semaphore_signal(barrier, inc=1, device_id=other, device_id_type=MESH)

    meanwhile()
    pl.semaphore_wait(barrier, count)


def pick(index, values):
    result = values[-1]
    for i, value in enumerate(values[:-1]):
        result = jnp.where(index == i, value, result)
    return result


def kernel(
    names, dims, group, toks, bounds, gain, q, k, v, r, gate_all, up_all, down_all, out, *scratch
):
    c = SimpleNamespace(**dims, **dict(zip(names, scratch)))
    tok, column = lax.axis_index("tok"), lax.axis_index("head")
    parity = tok % 2
    peers, rows, width = 2 * group, c.rows, c.width
    half, part = group // 2, rows // 2
    side = column // half
    me = parity * group + column
    first_late = group
    after = ((tok + 2) % toks, column)
    before = ((tok + toks - 2) % toks, column)
    has_after, has_before = tok < toks - 2, tok >= 2
    c.feature = 2 * column + parity
    c.bound = bounds[tok // 2]
    c.first_segment = jnp.where(tok < 2, 1, 0)
    loads = [
        pltpu.make_async_copy(source, mine, c.w_sem.at[i])
        for i, (source, mine) in enumerate(
            (
                (r, c.my_rates),
                (gain, c.gain),
                (gate_all.at[parity], c.wg),
                (up_all.at[parity], c.wu),
                (down_all.at[parity], c.wd),
            )
        )
    ]

    def columns(peer):
        return at(feature_of(peer, group) * width, width, width)

    def slot(t, start, size):
        return (c.k, c.v, c.q)[t].at[at((WINDOW if t < 2 else 0) + start, size, 128), :]

    owns = [
        pltpu.make_async_copy((k, v, q)[t].at[:, columns(me)], slot(t, me * rows, rows), c.own_sem.at[t])
        for t in range(3)
    ]

    def load():
        for copy in loads + owns:
            copy.start()
        loads[0].wait()
        c.rates[me] = c.my_rates[...]

    everybody = [place_of(flip(me, d, peers), tok, group) for d in range(1, peers)]
    greet(everybody, ((has_after, after), (has_before, before)), load)

    def remote(source, target, send, recv, peer):
        return pltpu.make_async_remote_copy(
            source, target, send, recv, device_id=place_of(peer, tok, group), device_id_type=MESH
        )

    def kv_copy(t, h, peer):
        return remote(
            (k, v)[t].at[pl.ds(h * part, part), columns(peer)],
            slot(t, me * rows + h * part, part),
            c.kv_send.at[t, h, peer], c.kv_recv.at[t, h, me], peer,
        )

    def q_copy(peer):
        return remote(
            q.at[:, columns(peer)], slot(2, me * rows, rows), c.q_send.at[peer], c.q_recv.at[me], peer
        )

    def rate_copy(peer):
        return remote(c.my_rates, c.rates.at[me], c.rate_send.at[peer], c.rate_recv.at[me], peer)

    def got_kv(peer, h):
        @pl.when(me != peer)
        def _():
            for t in range(2):
                target = slot(t, peer * rows + h * part, part)
                remote(target, target, c.kv_send.at[t, h, peer], c.kv_recv.at[t, h, peer], peer).wait_recv()

    def got_q(peer):
        @pl.when(me != peer)
        def _():
            target = slot(2, peer * rows, rows)
            remote(target, target, c.q_send.at[peer], c.q_recv.at[peer], peer).wait_recv()

    def got_rates(peer):
        @pl.when(me != peer)
        def _():
            target = c.rates.at[peer]
            remote(target, target, c.rate_send.at[peer], c.rate_recv.at[peer], peer).wait_recv()

    def block(peer):
        return out.at[:, columns(peer)]

    def done_rows(peer):
        return c.out.at[at(peer * rows, rows, rows), :]

    def give(peer):
        return remote(done_rows(peer), block(me), c.out_send.at[peer], c.out_recv.at[me], peer)

    def taken(peer):
        return remote(done_rows(peer), block(peer), c.out_send.at[peer], c.out_recv.at[peer], peer)

    keep = pltpu.make_async_copy(done_rows(me), block(me), c.out_own)

    def hand_out(peer):
        @pl.when(peer != me)
        def _():
            give(peer).start()

        @pl.when(peer == me)
        def _():
            keep.start()

    halos = [
        pltpu.make_async_remote_copy(
            o.at[pl.ds(c.length, WINDOW), :], o.at[pl.ds(0, WINDOW), :],
            c.halo_send.at[t], c.halo_recv.at[t], device_id=after, device_id_type=MESH,
        )
        for t, o in enumerate((c.k, c.v))
    ]

    chip = list(range(1, half))
    along = list(range(half, group))
    across = list(range(group, group + half))
    corner = list(range(group + half, peers))
    near = [d for pair in zip(along, across) for d in pair]
    everyone = chip + near + corner

    def send_kv(ds, hs=(0, 1), owner=True):
        for d in ds:
            for h in hs:
                def start():
                    for t in range(2):
                        kv_copy(t, h, flip(me, d, peers)).start()

                if h == 0 and owner:
                    pl.when(me != first_late)(start)
                else:
                    start()

    def send_q(ds):
        for d in ds:
            q_copy(flip(me, d, peers)).start()

    has_rates = (parity == 0) | (me == first_late)

    @pl.when(has_rates)
    def _():
        for d in everyone:
            rate_copy(flip(me, d, peers)).start()

    @pl.when(me == first_late)
    def _():
        send_kv(corner + near + chip, (0,), False)

    send_kv(chip + near)
    send_q(chip)

    @pl.when(parity == 1)
    def _():
        send_q(near)

    def send_corner():
        send_kv(corner)
        send_q(corner)

    pl.when((parity == 0) | (side == 0))(send_corner)

    @pl.when(parity == 0)
    def _():
        send_q(along)

    for copy in loads[1:] + owns:
        copy.wait()
    transpose_down(c)
    clear_gradients(c)
    measure_start(c)

    @pl.when(tok < 2)
    def _():
        c.k[:WINDOW, :] = jnp.zeros((WINDOW, width), BF16)
        c.v[:WINDOW, :] = jnp.zeros((WINDOW, width), BF16)

    tiles = rows // (WINDOW // 2)

    def got_first_late():
        got_kv(first_late, 1)
        for p in range(group + 1, group + half):
            for h in range(2):
                got_kv(p, h)

    def got_last():
        for p in range(group + half, peers):
            for h in range(2):
                got_kv(p, h)
        for halo in halos:
            pl.when(has_after)(halo.start)

    def block_of(quarter, j):
        return quarter * half + (j + column) % half

    def attend(quarter, j):
        peer = block_of(quarter, j)
        got_q(peer)

        @pl.when((quarter == 0) & (j == 0) & has_before)
        def _():
            for halo in halos:
                halo.wait_recv()

        attention(c, peer * tiles, tiles)

    def train(i):
        p = flip_by(column, i, group)
        got_rates(p)
        for h in range(2):
            got_kv(p, h)
        train_rows(c, p, p * rows, rows)

        @pl.when(i == half - 1)
        def _():
            got_rates(first_late)
            got_kv(first_late, 0)
            train_rows(c, first_late, c.length // 2, part)

            @pl.when(parity == 1)
            def _():
                @pl.when(side == 1)
                def _():
                    for d in along:
                        q_copy(flip(me, d, peers)).wait_send()
                    send_corner()

                got_first_late()
                got_last()

        @pl.when((parity == 1) & ((i == half - 1) | ((i == half) & (side == 1))))
        def _():
            loop(half, lambda j: attend(half + 2 - i, j))

    loop(group, train)

    @pl.when((parity == 0) & (side == 0))
    def _():
        got_first_late()

    @pl.when((parity == 0) & (side == 1))
    def _():
        got_last()

    scale_gradients(c)
    for turn in range(NS_ITERS):
        sweep(c, turn)

        if turn == 1:

            @pl.when(parity == 1)
            def _():
                def step(j):
                    peer = block_of(1 - side, j)
                    attend(1 - side, j)
                    fast_old(c, peer)
                    pl.when(peer != group - 1)(functools.partial(hand_out, peer))

                loop(half, step)

    renorm(c)

    def last(step):
        s, j = step // half, step % half
        early = jnp.where(side == 0, pick(s, (2, 1, 3, 0)), pick(s, (1, 3, 0, 2)))
        late = pick(s, (3 - side, side, 2 + side))
        quarter = jnp.where(parity == 0, early, late)

        peer = block_of(quarter, j)

        @pl.when((parity == 0) & (s == 1) & (j == 0))
        def _():
            pl.when(side == 0)(got_last)
            pl.when(side == 1)(got_first_late)
            send_q(across)

            @pl.when(side == 0)
            def _():
                for i in range(half):
                    hand_out(2 * half + i)

        @pl.when((parity == 0) | (s == 1) | ((s == 2) & (side == 0)))
        def _():
            attend(quarter, j)

        @pl.when(quarter < 2)
        def _():
            fast_old(c, peer)

        @pl.when(quarter >= 2)
        def _():
            fast_new(c, peer)

        now = (peer != group - 1) & ((parity == 1) | (side == 1) | (s > 0))
        pl.when(now)(functools.partial(hand_out, peer))
        late_edge = (parity == 1) & (side == 0) & (s == 0) & (j == half - 1)

        @pl.when((peer == group - 1) | late_edge)
        def _():
            close_edge(c)
            hand_out(group - 1)

    loop(jnp.where(parity == 0, 4, 3) * half, last)
    keep.wait()
    for d in everyone:
        taken(flip(me, d, peers)).wait_recv()
    for d in everyone:
        peer = flip(me, d, peers)
        give(peer).wait_send()
        if d in along:
            pl.when((parity == 0) | (side == 0))(q_copy(peer).wait_send)
        else:
            q_copy(peer).wait_send()
        for t in range(2):
            for h in range(2):
                kv_copy(t, h, peer).wait_send()
    for halo in halos:
        pl.when(has_after)(halo.wait_send)

    @pl.when(has_rates)
    def _():
        for d in everyone:
            rate_copy(flip(me, d, peers)).wait_send()


def body(queries, keys, values, token_rates, gate_start, up_start, down_start, norm_gain, bounds):
    rows, feats = queries.shape
    group, toks = lax.axis_size("head"), lax.axis_size("tok")
    heads, width, hid_width = token_rates.shape[1], gate_start.shape[1], gate_start.shape[2]
    peers = 2 * group
    length = peers * rows
    anywhere = pl.BlockSpec(memory_space=pl.ANY)
    scratch = scratch_of(length, width, hid_width, rows, peers)
    return pl.pallas_call(
        functools.partial(
            kernel, tuple(scratch), sizes(length, width, hid_width, rows), group, toks
        ),
        out_shape=jax.ShapeDtypeStruct((rows, feats), BF16),
        in_specs=[pl.BlockSpec(memory_space=pltpu.SMEM)] + [anywhere] * 8,
        out_specs=anywhere,
        scratch_shapes=list(scratch.values()),
        compiler_params=pltpu.CompilerParams(
            collective_id=0, has_side_effects=True, vmem_limit_bytes=66000000
        ),
        name="layer",
    )(
        bounds, norm_gain.reshape(heads, 1, width), queries, keys, values, token_rates.T,
        gate_start, up_start, down_start,
    )


def solution(mesh):
    spread = P(("tok", "head"), None)
    owned = P("head", None, None)
    return jax.shard_map(
        body,
        mesh=mesh,
        in_specs=(spread,) * 4 + (owned,) * 3 + (P(), P()),
        out_specs=spread,
        check_vma=False,
    )
```

```python
import functools
import math
from types import SimpleNamespace

import jax
import jax.numpy as jnp
from jax import lax
from jax.experimental import pallas as pl
from jax.experimental.pallas import tpu as pltpu
from jax.sharding import PartitionSpec as P

AHD = 128
WINDOW = 512
NS_ITERS = 3
CHUNK = 512

linear_coef = 3.4445
cubic_coef = -4.775
quintic_coef = 2.0315
rms_epsilon = 1e-05
norm_epsilon = 1e-06
MESH = pl.DeviceIdType.MESH
F32 = jnp.float32
BF16 = jnp.bfloat16


def mm(a, b, ca=1, cb=0):
    return lax.dot_general(a, b, (((ca,), (cb,)), ((), ())), preferred_element_type=F32)


def logistic(x):
    return 0.5 * jnp.tanh(0.5 * x) + 0.5


def loop(count, fn):
    def step(i, carry):
        fn(i)
        return carry

    lax.fori_loop(0, count, step, 0)


def at(start, size, multiple):
    return pl.ds(pl.multiple_of(start, multiple), size)


def transpose_down(c):
    def step(i):
        cols = at(i * CHUNK, CHUNK, CHUNK)
        c.wdt[:, cols] = c.wd[cols, :].T

    loop(c.hid_width // CHUNK, step)


def clear_gradients(c):
    def step(i):
        c.grad[:, at(i * 64, 64, 64), :] = jnp.zeros((3, 64, c.hid_width), F32)

    loop(c.width // 64, step)


def train_rows(c, block, start, size):
    for i in range(size // 128):
        part = slice(i * 128, (i + 1) * 128)
        here = at(WINDOW + start + i * 128, 128, 128)
        rates = c.rates[block, :, part].astype(F32)
        mine = lax.broadcasted_iota(jnp.int32, rates.shape, 0) == c.feature
        rates = jnp.sum(jnp.where(mine, rates, 0.0), axis=0, keepdims=True)
        rate_col = jnp.broadcast_to(rates, (128, 128)).T[:, 0:1]
        place = start + i * 128 + lax.broadcasted_iota(jnp.int32, (128, c.width), 0)
        target = jnp.where(place < c.bound, rate_col * c.v[here, :].astype(F32), 0.0)
        c.target[part, :] = target.astype(BF16)
        c.target_t[:, part] = target.T.astype(BF16)
        c.k_t[:, part] = c.k[here, :].T
    k_rows = c.k[at(WINDOW + start, size, 128), :]
    for i in range(c.hid_width // CHUNK):
        cols = slice(i * CHUNK, (i + 1) * CHUNK)
        gate = mm(k_rows, c.wg[:, cols])
        up = mm(k_rows, c.wu[:, cols])
        sig = logistic(gate)
        act = gate * sig
        slope = up * (sig + act * (1.0 - sig))
        back = mm(c.target[:size, :], c.wdt[:, cols])
        lefts = (c.k_t, c.k_t, c.target_t)
        rights = (back * slope, back * act, act * up)
        for m, (left, right) in enumerate(zip(lefts, rights)):
            total = c.grad[m, :, cols] + mm(left[:, :size], right.astype(BF16))
            c.grad[m, :, cols] = total
            c.squares[m, :, cols] = jnp.sum((total * total).reshape(-1, 8, CHUNK), axis=0)


def scale_gradients(c):
    for m in range(3):
        frob = lax.rsqrt(jnp.sum(c.squares[m], keepdims=True) + norm_epsilon)
        c.x[0, m] = (c.grad[m] * frob).astype(BF16)


def symmetric(ref, m, size, top, corner):
    ref[m, :size, :] = top
    ref[m, size:, size:] = corner
    ref[m, size:, :size] = top[:, size:].T


def sweep(c, turn):
    old, new, h = turn % 2, (turn + 1) % 2, c.width // 2
    for m in range(3):
        x = c.x[old, m]
        top, corner = mm(x[:h], x, 1, 1), mm(x[h:], x[h:], 1, 1)
        symmetric(c.a, m, h, top.astype(BF16), corner.astype(BF16))
    for m in range(3):
        a = c.a[m]
        top = cubic_coef * a[:h].astype(F32) + quintic_coef * mm(a[:h], a)
        corner = cubic_coef * a[h:, h:].astype(F32) + quintic_coef * mm(a[h:], a[:, h:])
        symmetric(c.p, m, h, top.astype(BF16), corner.astype(BF16))
    for m in range(3):
        x = c.x[old, m]
        c.x[new, m] = (linear_coef * x.astype(F32) + mm(c.p[m], x)).astype(BF16)


def measure_start(c):
    for m, ref in ((0, c.wg), (1, c.wu)):
        for i in range(c.hid_width // CHUNK):
            cols = slice(i * CHUNK, (i + 1) * CHUNK)
            w = ref[:, cols].astype(F32)
            c.want[m, :, cols] = jnp.sqrt(jnp.sum(w * w, axis=0, keepdims=True) + norm_epsilon)

    def by_row(i):
        rows = at(i * 128, 128, 128)
        w = c.wdt[rows, :].astype(F32)
        c.want_down[rows, :] = jnp.sqrt(jnp.sum(w * w, axis=1, keepdims=True) + norm_epsilon)

    loop(c.width // 128, by_row)


def renorm(c):
    x = c.x.at[NS_ITERS % 2]
    for m, ref in ((0, c.wg), (1, c.wu)):
        for i in range(c.hid_width // CHUNK):
            cols = slice(i * CHUNK, (i + 1) * CHUNK)
            u = ref[:, cols].astype(F32) + x[m, :, cols].astype(F32)
            have = lax.rsqrt(jnp.sum(u * u, axis=0, keepdims=True) + norm_epsilon)
            x[m, :, cols] = (u * (c.want[m, :, cols] * have)).astype(BF16)
    for i in range(c.width // 128):
        rows = slice(i * 128, (i + 1) * 128)
        u = c.wdt[rows, :].astype(F32) + x[2, rows, :].astype(F32)
        have = lax.rsqrt(jnp.sum(u * u, axis=1, keepdims=True) + norm_epsilon)
        x[2, rows, :] = (u * (c.want_down[rows, :] * have)).astype(BF16)


def attention(c, first, count):
    tile = WINDOW // 2
    power = math.log2(math.e) / math.sqrt(AHD)

    def step(i):
        t = first + i
        rows = at(t * tile, tile, tile)
        span = at(t * tile, WINDOW + tile, tile)
        below = lax.broadcasted_iota(jnp.int32, (tile, tile), 1) <= lax.broadcasted_iota(
            jnp.int32, (tile, tile), 0
        )
        far_bias = jnp.where(c.first_segment * (2 - t) > 0, F32(-1e30), F32(0.0))
        mid_bias = jnp.where(c.first_segment * (1 - t) > 0, F32(-1e30), F32(0.0))
        for head in range(c.width // AHD):
            feats = slice(head * AHD, (head + 1) * AHD)
            scores = mm(c.q[rows, feats], c.k[span, feats], 1, 1)
            edge = jnp.where(below, scores[:, 2 * tile :], scores[:, :tile] + far_bias)
            mid = scores[:, tile : 2 * tile] + mid_bias
            top = jnp.max(jnp.maximum(edge, mid), axis=1, keepdims=True)
            edge = jnp.exp2((edge - top) * power)
            mid = jnp.exp2((mid - top) * power)
            total = jnp.sum(edge + mid, axis=1, keepdims=True)
            weights = jnp.concatenate(
                [
                    jnp.where(below, 0.0, edge).astype(BF16),
                    mid.astype(BF16),
                    jnp.where(below, edge, 0.0).astype(BF16),
                ],
                axis=1,
            )
            mixed = mm(weights, c.v[span, feats])
            c.out[rows, feats] = (mixed / total).astype(BF16)

    loop(count, step)


def swiglu(c, start, size, gate, up, down, down_dim):
    q_rows = c.q[at(start, size, 128), :]
    for i in range(c.hid_width // CHUNK):
        cols = slice(i * CHUNK, (i + 1) * CHUNK)
        pre_gate = mm(q_rows, gate[:, cols])
        pre_up = mm(q_rows, up[:, cols])
        c.apply_hid[:size, cols] = (pre_gate * logistic(pre_gate) * pre_up).astype(BF16)
    return mm(c.apply_hid[:size, :], down[...], 1, down_dim)


def old_rows(c, start, size):
    return swiglu(c, start, size, c.wg, c.wu, c.wd, 0)


def new_rows(c, start, size):
    new = c.x.at[NS_ITERS % 2]
    return swiglu(c, start, size, new.at[0], new.at[1], new.at[2], 1)


def finish_rows(c, start, raw):
    rows = at(start, raw.shape[0], 128)
    scale = lax.rsqrt(jnp.mean(raw * raw, axis=1, keepdims=True) + rms_epsilon)
    fast = (raw * scale * c.gain[c.feature]).astype(BF16)
    c.out[rows, :] = (c.out[rows, :].astype(F32) + fast.astype(F32)).astype(BF16)


def below_bound(c, start, shape):
    return start + lax.broadcasted_iota(jnp.int32, shape, 0) < c.bound


def fast_old(c, block):
    size = c.rows // 2
    start = block * c.rows
    c.raw[...] = old_rows(c, start, c.rows)
    finish_rows(c, start, c.raw[:size, :])

    @pl.when(start + c.rows <= c.low)
    def _():
        finish_rows(c, start + size, c.raw[size:, :])

    @pl.when(start + c.rows > c.low)
    def _():
        c.open_raw[...] = c.raw[size:, :]


def close_edge(c):
    after = new_rows(c, c.low, c.rows // 2)
    finish_rows(c, c.low, jnp.where(below_bound(c, c.low, after.shape), c.open_raw[...], after))


def fast_new(c, block):
    size = c.rows // 2
    start = block * c.rows
    c.raw[...] = new_rows(c, start, c.rows)

    @pl.when(start < c.high)
    def _():
        before = old_rows(c, start, size)
        after = c.raw[:size, :]
        c.raw[:size, :] = jnp.where(below_bound(c, start, after.shape), before, after)

    finish_rows(c, start, c.raw[...])


def scratch_of(length, width, hid_width, rows, peers, segments):
    dma = pltpu.SemaphoreType.DMA
    return {
        "q": pltpu.VMEM((length, width), BF16),
        "k": pltpu.VMEM((WINDOW + length, width), BF16),
        "v": pltpu.VMEM((WINDOW + length, width), BF16),
        "my_rates": pltpu.VMEM((peers, rows), BF16),
        "rates": pltpu.VMEM((peers, peers, rows), BF16),
        "gain": pltpu.VMEM((peers, 1, width), F32),
        "bounds": pltpu.SMEM(segments, jnp.int32),
        "out": pltpu.VMEM((length, width), BF16),
        "kv_send": dma((2, 2, peers)),
        "kv_recv": dma((2, 2, peers)),
        "q_send": dma((peers,)),
        "q_recv": dma((peers,)),
        "rate_send": dma((peers,)),
        "rate_recv": dma((peers,)),
        "own_sem": dma((3,)),
        "halo_send": dma((2,)),
        "halo_recv": dma((2,)),
        "out_send": dma((peers,)),
        "out_recv": dma((peers,)),
        "out_own": dma,
        "wg": pltpu.VMEM((width, hid_width), BF16),
        "wu": pltpu.VMEM((width, hid_width), BF16),
        "wd": pltpu.VMEM((hid_width, width), BF16),
        "wdt": pltpu.VMEM((width, hid_width), BF16),
        "target": pltpu.VMEM((rows, width), BF16),
        "target_t": pltpu.VMEM((width, rows), BF16),
        "k_t": pltpu.VMEM((width, rows), BF16),
        "grad": pltpu.VMEM((3, width, hid_width), F32),
        "squares": pltpu.VMEM((3, 8, hid_width), F32),
        "want": pltpu.VMEM((2, 1, hid_width), F32),
        "want_down": pltpu.VMEM((width, 1), F32),
        "x": pltpu.VMEM((2, 3, width, hid_width), BF16),
        "a": pltpu.VMEM((3, width, width), BF16),
        "p": pltpu.VMEM((3, width, width), BF16),
        "apply_hid": pltpu.VMEM((rows, hid_width), BF16),
        "raw": pltpu.VMEM((rows, width), F32),
        "open_raw": pltpu.VMEM((rows // 2, width), F32),
        "w_sem": dma((6,)),
    }


def sizes(length, width, hid_width, rows):
    low, high = length // 2 - length // 16, length // 2 + length // 16
    return dict(
        length=length, width=width, hid_width=hid_width, rows=rows, low=low, high=high
    )


def flip(index, distance, count):
    result, place = 0, 1
    while place < count:
        bit = (index // place) % 2
        result = result + place * (1 - bit if distance & place else bit)
        place *= 2
    return result


def flip_by(index, distance, count):
    result, place = 0, 1
    while place < count:
        bit, other = (index // place) % 2, (distance // place) % 2
        result = result + place * (bit + other - 2 * bit * other)
        place *= 2
    return result


def place_of(peer, tok, group):
    return (tok - tok % 2 + peer // group, peer % group)


def feature_of(peer, group):
    return 2 * (peer % group) + peer // group


def greet(others, neighbours, meanwhile):
    barrier = pltpu.get_barrier_semaphore()
    count = len(others)
    for other in others:
        pl.semaphore_signal(barrier, inc=1, device_id=other, device_id_type=MESH)
    for exists, other in neighbours:
        count = count + jnp.where(exists, 1, 0)

        @pl.when(exists)
        def _(other=other):
            pl.semaphore_signal(barrier, inc=1, device_id=other, device_id_type=MESH)

    meanwhile()
    pl.semaphore_wait(barrier, count)


def pick(index, values):
    result = values[-1]
    for i, value in enumerate(values[:-1]):
        result = jnp.where(index == i, value, result)
    return result


def kernel(
    names, dims, group, toks, bounds, gain, q, k, v, r, gate_all, up_all, down_all, out, *scratch
):
    c = SimpleNamespace(**dims, **dict(zip(names, scratch)))
    tok, column = lax.axis_index("tok"), lax.axis_index("head")
    parity = tok % 2
    peers, rows, width = 2 * group, c.rows, c.width
    half, part = group // 2, rows // 2
    side = column // half
    me = parity * group + column
    first_late = group
    after = ((tok + 2) % toks, column)
    before = ((tok + toks - 2) % toks, column)
    has_after, has_before = tok < toks - 2, tok >= 2
    c.feature = 2 * column + parity
    c.first_segment = jnp.where(tok < 2, 1, 0)
    loads = [
        pltpu.make_async_copy(source, mine, c.w_sem.at[i])
        for i, (source, mine) in enumerate(
            (
                (r, c.my_rates),
                (bounds, c.bounds),
                (gain, c.gain),
                (gate_all.at[parity], c.wg),
                (up_all.at[parity], c.wu),
                (down_all.at[parity], c.wd),
            )
        )
    ]

    def columns(peer):
        return at(feature_of(peer, group) * width, width, width)

    def slot(t, start, size):
        return (c.k, c.v, c.q)[t].at[at((WINDOW if t < 2 else 0) + start, size, 128), :]

    owns = [
        pltpu.make_async_copy((k, v, q)[t].at[:, columns(me)], slot(t, me * rows, rows), c.own_sem.at[t])
        for t in range(3)
    ]

    def load():
        for copy in loads + owns:
            copy.start()
        loads[0].wait()
        c.rates[me] = c.my_rates[...]

    everybody = [place_of(flip(me, d, peers), tok, group) for d in range(1, peers)]
    greet(everybody, ((has_after, after), (has_before, before)), load)

    def remote(source, target, send, recv, peer):
        return pltpu.make_async_remote_copy(
            source, target, send, recv, device_id=place_of(peer, tok, group), device_id_type=MESH
        )

    def kv_copy(t, h, peer):
        return remote(
            (k, v)[t].at[pl.ds(h * part, part), columns(peer)],
            slot(t, me * rows + h * part, part),
            c.kv_send.at[t, h, peer], c.kv_recv.at[t, h, me], peer,
        )

    def q_copy(peer):
        return remote(
            q.at[:, columns(peer)], slot(2, me * rows, rows), c.q_send.at[peer], c.q_recv.at[me], peer
        )

    def rate_copy(peer):
        return remote(c.my_rates, c.rates.at[me], c.rate_send.at[peer], c.rate_recv.at[me], peer)

    def got_kv(peer, h):
        @pl.when(me != peer)
        def _():
            for t in range(2):
                target = slot(t, peer * rows + h * part, part)
                remote(target, target, c.kv_send.at[t, h, peer], c.kv_recv.at[t, h, peer], peer).wait_recv()

    def got_q(peer):
        @pl.when(me != peer)
        def _():
            target = slot(2, peer * rows, rows)
            remote(target, target, c.q_send.at[peer], c.q_recv.at[peer], peer).wait_recv()

    def got_rates(peer):
        @pl.when(me != peer)
        def _():
            target = c.rates.at[peer]
            remote(target, target, c.rate_send.at[peer], c.rate_recv.at[peer], peer).wait_recv()

    def block(peer):
        return out.at[:, columns(peer)]

    def done_rows(peer):
        return c.out.at[at(peer * rows, rows, rows), :]

    def give(peer):
        return remote(done_rows(peer), block(me), c.out_send.at[peer], c.out_recv.at[me], peer)

    def taken(peer):
        return remote(done_rows(peer), block(peer), c.out_send.at[peer], c.out_recv.at[peer], peer)

    keep = pltpu.make_async_copy(done_rows(me), block(me), c.out_own)

    def hand_out(peer):
        @pl.when(peer != me)
        def _():
            give(peer).start()

        @pl.when(peer == me)
        def _():
            keep.start()

    halos = [
        pltpu.make_async_remote_copy(
            o.at[pl.ds(c.length, WINDOW), :], o.at[pl.ds(0, WINDOW), :],
            c.halo_send.at[t], c.halo_recv.at[t], device_id=after, device_id_type=MESH,
        )
        for t, o in enumerate((c.k, c.v))
    ]

    chip = list(range(1, half))
    along = list(range(half, group))
    across = list(range(group, group + half))
    corner = list(range(group + half, peers))
    near = [d for pair in zip(along, across) for d in pair]
    everyone = chip + near + corner

    def send_kv(ds, hs=(0, 1), owner=True):
        for d in ds:
            for h in hs:
                def start():
                    for t in range(2):
                        kv_copy(t, h, flip(me, d, peers)).start()

                if h == 0 and owner:
                    pl.when(me != first_late)(start)
                else:
                    start()

    def send_q(ds):
        for d in ds:
            q_copy(flip(me, d, peers)).start()

    has_rates = (parity == 0) | (me == first_late)

    @pl.when(has_rates)
    def _():
        for d in everyone:
            rate_copy(flip(me, d, peers)).start()

    @pl.when(me == first_late)
    def _():
        send_kv(corner + near + chip, (0,), False)

    send_kv(chip + near)
    send_q(chip)

    @pl.when(parity == 1)
    def _():
        send_q(near)

    def send_corner():
        send_kv(corner)
        send_q(corner)

    pl.when((parity == 0) | (side == 0))(send_corner)

    @pl.when(parity == 0)
    def _():
        send_q(along)

    for copy in loads[1:] + owns:
        copy.wait()
    c.bound = c.bounds[tok // 2]
    transpose_down(c)
    clear_gradients(c)
    measure_start(c)

    @pl.when(tok < 2)
    def _():
        c.k[:WINDOW, :] = jnp.zeros((WINDOW, width), BF16)
        c.v[:WINDOW, :] = jnp.zeros((WINDOW, width), BF16)

    tiles = rows // (WINDOW // 2)

    def got_first_late():
        got_kv(first_late, 1)
        for p in range(group + 1, group + half):
            for h in range(2):
                got_kv(p, h)

    def got_last():
        for p in range(group + half, peers):
            for h in range(2):
                got_kv(p, h)
        for halo in halos:
            pl.when(has_after)(halo.start)

    def block_of(quarter, j):
        return quarter * half + (j + column) % half

    def attend(quarter, j):
        peer = block_of(quarter, j)
        got_q(peer)

        @pl.when((quarter == 0) & (j == 0) & has_before)
        def _():
            for halo in halos:
                halo.wait_recv()

        attention(c, peer * tiles, tiles)

    def train(i):
        p = flip_by(column, i, group)
        got_rates(p)
        for h in range(2):
            got_kv(p, h)
        train_rows(c, p, p * rows, rows)

        @pl.when(i == half - 1)
        def _():
            got_rates(first_late)
            got_kv(first_late, 0)
            train_rows(c, first_late, c.length // 2, part)

            @pl.when(parity == 1)
            def _():
                @pl.when(side == 1)
                def _():
                    for d in along:
                        q_copy(flip(me, d, peers)).wait_send()
                    send_corner()

                got_first_late()
                got_last()

        @pl.when((parity == 1) & ((i == half - 1) | ((i == half) & (side == 1))))
        def _():
            loop(half, lambda j: attend(half + 2 - i, j))

    loop(group, train)

    @pl.when((parity == 0) & (side == 0))
    def _():
        got_first_late()

    @pl.when((parity == 0) & (side == 1))
    def _():
        got_last()

    scale_gradients(c)
    for turn in range(NS_ITERS):
        sweep(c, turn)

        if turn == 1:

            @pl.when(parity == 1)
            def _():
                def step(j):
                    peer = block_of(1 - side, j)
                    attend(1 - side, j)
                    fast_old(c, peer)
                    pl.when(peer != group - 1)(functools.partial(hand_out, peer))

                loop(half, step)

    renorm(c)

    def last(step):
        s, j = step // half, step % half
        early = jnp.where(side == 0, pick(s, (2, 1, 3, 0)), pick(s, (1, 3, 0, 2)))
        late = pick(s, (3 - side, side, 2 + side))
        quarter = jnp.where(parity == 0, early, late)

        peer = block_of(quarter, j)

        @pl.when((parity == 0) & (s == 1) & (j == 0))
        def _():
            pl.when(side == 0)(got_last)
            pl.when(side == 1)(got_first_late)
            send_q(across)

            @pl.when(side == 0)
            def _():
                for i in range(half):
                    hand_out(2 * half + i)

        @pl.when((parity == 0) | (s == 1) | ((s == 2) & (side == 0)))
        def _():
            attend(quarter, j)

        @pl.when(quarter < 2)
        def _():
            fast_old(c, peer)

        @pl.when(quarter >= 2)
        def _():
            fast_new(c, peer)

        now = (peer != group - 1) & ((parity == 1) | (side == 1) | (s > 0))
        pl.when(now)(functools.partial(hand_out, peer))
        late_edge = (parity == 1) & (side == 0) & (s == 0) & (j == half - 1)

        @pl.when((peer == group - 1) | late_edge)
        def _():
            close_edge(c)
            hand_out(group - 1)

    loop(jnp.where(parity == 0, 4, 3) * half, last)
    keep.wait()
    for d in everyone:
        taken(flip(me, d, peers)).wait_recv()
    for d in everyone:
        peer = flip(me, d, peers)
        give(peer).wait_send()
        if d in along:
            pl.when((parity == 0) | (side == 0))(q_copy(peer).wait_send)
        else:
            q_copy(peer).wait_send()
        for t in range(2):
            for h in range(2):
                kv_copy(t, h, peer).wait_send()
    for halo in halos:
        pl.when(has_after)(halo.wait_send)

    @pl.when(has_rates)
    def _():
        for d in everyone:
            rate_copy(flip(me, d, peers)).wait_send()


def body(queries, keys, values, token_rates, gate_start, up_start, down_start, norm_gain, bounds):
    rows, feats = queries.shape
    group, toks = lax.axis_size("head"), lax.axis_size("tok")
    heads, width, hid_width = token_rates.shape[1], gate_start.shape[1], gate_start.shape[2]
    peers = 2 * group
    length = peers * rows
    scratch = scratch_of(length, width, hid_width, rows, peers, bounds.shape)
    return pl.pallas_call(
        functools.partial(
            kernel, tuple(scratch), sizes(length, width, hid_width, rows), group, toks
        ),
        out_shape=jax.ShapeDtypeStruct((rows, feats), BF16),
        in_specs=[pl.BlockSpec(memory_space=pltpu.HBM)] * 9,
        out_specs=pl.BlockSpec(memory_space=pl.ANY),
        scratch_shapes=list(scratch.values()),
        compiler_params=pltpu.CompilerParams(
            collective_id=0, has_side_effects=True, vmem_limit_bytes=50000000
        ),
        name="layer",
    )(
        *(
            pltpu.with_memory_space_constraint(x, pltpu.HBM)
            for x in (
                bounds, norm_gain.reshape(heads, 1, width), queries, keys, values, token_rates.T,
                gate_start, up_start, down_start,
            )
        )
    )


def solution(mesh):
    spread = P(("tok", "head"), None)
    owned = P("head", None, None)
    return jax.shard_map(
        body,
        mesh=mesh,
        in_specs=(spread,) * 4 + (owned,) * 3 + (P(), P()),
        out_specs=spread,
        check_vma=False,
    )
```

```python
import functools
import math
from types import SimpleNamespace

import jax
import jax.numpy as jnp
from jax import lax
from jax.experimental import pallas as pl
from jax.experimental.pallas import tpu as pltpu
from jax.sharding import PartitionSpec as P

AHD = 128
WINDOW = 512
NS_ITERS = 3
CHUNK = 512

linear_coef = 3.4445
cubic_coef = -4.775
quintic_coef = 2.0315
rms_epsilon = 1e-05
norm_epsilon = 1e-06
MESH = pl.DeviceIdType.MESH
F32 = jnp.float32
BF16 = jnp.bfloat16


def mm(a, b, ca=1, cb=0):
    return lax.dot_general(a, b, (((ca,), (cb,)), ((), ())), preferred_element_type=F32)


def logistic(x):
    return 0.5 * jnp.tanh(0.5 * x) + 0.5


def loop(count, fn):
    def step(i, carry):
        fn(i)
        return carry

    lax.fori_loop(0, count, step, 0)


def at(start, size, multiple):
    return pl.ds(pl.multiple_of(start, multiple), size)


def transpose_down(c):
    def step(i):
        cols = at(i * CHUNK, CHUNK, CHUNK)
        c.wdt[:, cols] = c.wd[cols, :].T

    loop(c.hid_width // CHUNK, step)


def clear_gradients(c):
    def step(i):
        c.grad[:, at(i * 64, 64, 64), :] = jnp.zeros((3, 64, c.hid_width), F32)

    loop(c.width // 64, step)


def train_rows(c, block, start, size):
    for i in range(size // 128):
        part = slice(i * 128, (i + 1) * 128)
        here = at(WINDOW + start + i * 128, 128, 128)
        rates = c.rates[block, :, part].astype(F32)
        mine = lax.broadcasted_iota(jnp.int32, rates.shape, 0) == c.feature
        rates = jnp.sum(jnp.where(mine, rates, 0.0), axis=0, keepdims=True)
        rate_col = jnp.broadcast_to(rates, (128, 128)).T[:, 0:1]
        place = start + i * 128 + lax.broadcasted_iota(jnp.int32, (128, c.width), 0)
        target = jnp.where(place < c.bound, rate_col * c.v[here, :].astype(F32), 0.0)
        c.target[part, :] = target.astype(BF16)
        c.target_t[:, part] = target.T.astype(BF16)
        c.k_t[:, part] = c.k[here, :].T
    k_rows = c.k[at(WINDOW + start, size, 128), :]
    for i in range(c.hid_width // CHUNK):
        cols = slice(i * CHUNK, (i + 1) * CHUNK)
        gate = mm(k_rows, c.wg[:, cols])
        up = mm(k_rows, c.wu[:, cols])
        sig = logistic(gate)
        act = gate * sig
        slope = up * (sig + act * (1.0 - sig))
        back = mm(c.target[:size, :], c.wdt[:, cols])
        lefts = (c.k_t, c.k_t, c.target_t)
        rights = (back * slope, back * act, act * up)
        for m, (left, right) in enumerate(zip(lefts, rights)):
            total = c.grad[m, :, cols] + mm(left[:, :size], right.astype(BF16))
            c.grad[m, :, cols] = total
            c.squares[m, :, cols] = jnp.sum((total * total).reshape(-1, 8, CHUNK), axis=0)


def scale_gradients(c):
    for m in range(3):
        frob = lax.rsqrt(jnp.sum(c.squares[m], keepdims=True) + norm_epsilon)
        c.x[0, m] = (c.grad[m] * frob).astype(BF16)


def symmetric(ref, m, size, top, corner):
    ref[m, :size, :] = top
    ref[m, size:, size:] = corner
    ref[m, size:, :size] = top[:, size:].T


def sweep(c, turn):
    old, new, h = turn % 2, (turn + 1) % 2, c.width // 2
    for m in range(3):
        x = c.x[old, m]
        top, corner = mm(x[:h], x, 1, 1), mm(x[h:], x[h:], 1, 1)
        symmetric(c.a, m, h, top.astype(BF16), corner.astype(BF16))
    for m in range(3):
        a = c.a[m]
        top = cubic_coef * a[:h].astype(F32) + quintic_coef * mm(a[:h], a)
        corner = cubic_coef * a[h:, h:].astype(F32) + quintic_coef * mm(a[h:], a[:, h:])
        symmetric(c.p, m, h, top.astype(BF16), corner.astype(BF16))
    for m in range(3):
        x = c.x[old, m]
        c.x[new, m] = (linear_coef * x.astype(F32) + mm(c.p[m], x)).astype(BF16)


def measure_start(c):
    for m, ref in ((0, c.wg), (1, c.wu)):
        for i in range(c.hid_width // CHUNK):
            cols = slice(i * CHUNK, (i + 1) * CHUNK)
            w = ref[:, cols].astype(F32)
            c.want[m, :, cols] = jnp.sqrt(jnp.sum(w * w, axis=0, keepdims=True) + norm_epsilon)

    def by_row(i):
        rows = at(i * 128, 128, 128)
        w = c.wdt[rows, :].astype(F32)
        c.want_down[rows, :] = jnp.sqrt(jnp.sum(w * w, axis=1, keepdims=True) + norm_epsilon)

    loop(c.width // 128, by_row)


def renorm(c):
    x = c.x.at[NS_ITERS % 2]
    for m, ref in ((0, c.wg), (1, c.wu)):
        for i in range(c.hid_width // CHUNK):
            cols = slice(i * CHUNK, (i + 1) * CHUNK)
            u = ref[:, cols].astype(F32) + x[m, :, cols].astype(F32)
            have = lax.rsqrt(jnp.sum(u * u, axis=0, keepdims=True) + norm_epsilon)
            x[m, :, cols] = (u * (c.want[m, :, cols] * have)).astype(BF16)
    for i in range(c.width // 128):
        rows = slice(i * 128, (i + 1) * 128)
        u = c.wdt[rows, :].astype(F32) + x[2, rows, :].astype(F32)
        have = lax.rsqrt(jnp.sum(u * u, axis=1, keepdims=True) + norm_epsilon)
        x[2, rows, :] = (u * (c.want_down[rows, :] * have)).astype(BF16)


def attention(c, first, count):
    tile = WINDOW // 2
    power = math.log2(math.e) / math.sqrt(AHD)

    def step(i):
        t = first + i
        rows = at(t * tile, tile, tile)
        span = at(t * tile, WINDOW + tile, tile)
        below = lax.broadcasted_iota(jnp.int32, (tile, tile), 1) <= lax.broadcasted_iota(
            jnp.int32, (tile, tile), 0
        )
        far_bias = jnp.where(c.first_segment * (2 - t) > 0, F32(-1e30), F32(0.0))
        mid_bias = jnp.where(c.first_segment * (1 - t) > 0, F32(-1e30), F32(0.0))
        for head in range(c.width // AHD):
            feats = slice(head * AHD, (head + 1) * AHD)
            scores = mm(c.q[rows, feats], c.k[span, feats], 1, 1)
            edge = jnp.where(below, scores[:, 2 * tile :], scores[:, :tile] + far_bias)
            mid = scores[:, tile : 2 * tile] + mid_bias
            top = jnp.max(jnp.maximum(edge, mid), axis=1, keepdims=True)
            edge = jnp.exp2((edge - top) * power)
            mid = jnp.exp2((mid - top) * power)
            total = jnp.sum(edge + mid, axis=1, keepdims=True)
            weights = jnp.concatenate(
                [
                    jnp.where(below, 0.0, edge).astype(BF16),
                    mid.astype(BF16),
                    jnp.where(below, edge, 0.0).astype(BF16),
                ],
                axis=1,
            )
            mixed = mm(weights, c.v[span, feats])
            c.out[rows, feats] = (mixed / total).astype(BF16)

    loop(count, step)


def swiglu(c, start, size, gate, up, down, down_dim):
    q_rows = c.q[at(start, size, 128), :]
    for i in range(c.hid_width // CHUNK):
        cols = slice(i * CHUNK, (i + 1) * CHUNK)
        pre_gate = mm(q_rows, gate[:, cols])
        pre_up = mm(q_rows, up[:, cols])
        c.apply_hid[:size, cols] = (pre_gate * logistic(pre_gate) * pre_up).astype(BF16)
    return mm(c.apply_hid[:size, :], down[...], 1, down_dim)


def old_rows(c, start, size):
    return swiglu(c, start, size, c.wg, c.wu, c.wd, 0)


def new_rows(c, start, size):
    new = c.x.at[NS_ITERS % 2]
    return swiglu(c, start, size, new.at[0], new.at[1], new.at[2], 1)


def finish_rows(c, start, raw):
    rows = at(start, raw.shape[0], 128)
    scale = lax.rsqrt(jnp.mean(raw * raw, axis=1, keepdims=True) + rms_epsilon)
    fast = (raw * scale * c.gain[c.feature]).astype(BF16)
    c.out[rows, :] = (c.out[rows, :].astype(F32) + fast.astype(F32)).astype(BF16)


def below_bound(c, start, shape):
    return start + lax.broadcasted_iota(jnp.int32, shape, 0) < c.bound


def fast_old(c, block):
    size = c.rows // 2
    start = block * c.rows
    c.raw[...] = old_rows(c, start, c.rows)
    finish_rows(c, start, c.raw[:size, :])

    @pl.when(start + c.rows <= c.low)
    def _():
        finish_rows(c, start + size, c.raw[size:, :])

    @pl.when(start + c.rows > c.low)
    def _():
        c.open_raw[...] = c.raw[size:, :]


def close_edge(c):
    after = new_rows(c, c.low, c.rows // 2)
    finish_rows(c, c.low, jnp.where(below_bound(c, c.low, after.shape), c.open_raw[...], after))


def fast_new(c, block):
    size = c.rows // 2
    start = block * c.rows
    c.raw[...] = new_rows(c, start, c.rows)

    @pl.when(start < c.high)
    def _():
        before = old_rows(c, start, size)
        after = c.raw[:size, :]
        c.raw[:size, :] = jnp.where(below_bound(c, start, after.shape), before, after)

    finish_rows(c, start, c.raw[...])


def scratch_of(length, width, hid_width, rows, peers, segments):
    dma = pltpu.SemaphoreType.DMA
    return {
        "q": pltpu.VMEM((length, width), BF16),
        "k": pltpu.VMEM((WINDOW + length, width), BF16),
        "v": pltpu.VMEM((WINDOW + length, width), BF16),
        "my_rates": pltpu.VMEM((peers, rows), BF16),
        "rates": pltpu.VMEM((peers, peers, rows), BF16),
        "gain": pltpu.VMEM((peers, 1, width), F32),
        "bounds": pltpu.SMEM(segments, jnp.int32),
        "out": pltpu.VMEM((length, width), BF16),
        "kv_send": dma((2, 2, peers)),
        "kv_recv": dma((2, 2, peers)),
        "q_send": dma((peers,)),
        "q_recv": dma((peers,)),
        "rate_send": dma((peers,)),
        "rate_recv": dma((peers,)),
        "own_sem": dma((3,)),
        "halo_send": dma((2,)),
        "halo_recv": dma((2,)),
        "out_send": dma((peers,)),
        "out_recv": dma((peers,)),
        "out_own": dma,
        "wg": pltpu.VMEM((width, hid_width), BF16),
        "wu": pltpu.VMEM((width, hid_width), BF16),
        "wd": pltpu.VMEM((hid_width, width), BF16),
        "wdt": pltpu.VMEM((width, hid_width), BF16),
        "target": pltpu.VMEM((rows, width), BF16),
        "target_t": pltpu.VMEM((width, rows), BF16),
        "k_t": pltpu.VMEM((width, rows), BF16),
        "grad": pltpu.VMEM((3, width, hid_width), F32),
        "squares": pltpu.VMEM((3, 8, hid_width), F32),
        "want": pltpu.VMEM((2, 1, hid_width), F32),
        "want_down": pltpu.VMEM((width, 1), F32),
        "x": pltpu.VMEM((2, 3, width, hid_width), BF16),
        "a": pltpu.VMEM((3, width, width), BF16),
        "p": pltpu.VMEM((3, width, width), BF16),
        "apply_hid": pltpu.VMEM((rows, hid_width), BF16),
        "raw": pltpu.VMEM((rows, width), F32),
        "open_raw": pltpu.VMEM((rows // 2, width), F32),
        "w_sem": dma((6,)),
    }


def sizes(length, width, hid_width, rows):
    low, high = length // 2 - length // 16, length // 2 + length // 16
    return dict(
        length=length, width=width, hid_width=hid_width, rows=rows, low=low, high=high
    )


def flip(index, distance, count):
    result, place = 0, 1
    while place < count:
        bit = (index // place) % 2
        result = result + place * (1 - bit if distance & place else bit)
        place *= 2
    return result


def flip_by(index, distance, count):
    result, place = 0, 1
    while place < count:
        bit, other = (index // place) % 2, (distance // place) % 2
        result = result + place * (bit + other - 2 * bit * other)
        place *= 2
    return result


def place_of(peer, tok, group):
    return (tok - tok % 2 + peer // group, peer % group)


def feature_of(peer, group):
    return 2 * (peer % group) + peer // group


def greet(others, neighbours, meanwhile):
    barrier = pltpu.get_barrier_semaphore()
    count = len(others)
    for other in others:
        pl.semaphore_signal(barrier, inc=1, device_id=other, device_id_type=MESH)
    for exists, other in neighbours:
        count = count + jnp.where(exists, 1, 0)

        @pl.when(exists)
        def _(other=other):
            pl.semaphore_signal(barrier, inc=1, device_id=other, device_id_type=MESH)

    meanwhile()
    pl.semaphore_wait(barrier, count)


def pick(index, values):
    result = values[-1]
    for i, value in enumerate(values[:-1]):
        result = jnp.where(index == i, value, result)
    return result


def kernel(
    names, dims, group, toks, bounds, gain, q, k, v, r, gate_all, up_all, down_all, out, *scratch
):
    c = SimpleNamespace(**dims, **dict(zip(names, scratch)))
    tok, column = lax.axis_index("tok"), lax.axis_index("head")
    parity = tok % 2
    peers, rows, width = 2 * group, c.rows, c.width
    half, part = group // 2, rows // 2
    side = column // half
    me = parity * group + column
    first_late = group
    after = ((tok + 2) % toks, column)
    before = ((tok + toks - 2) % toks, column)
    has_after, has_before = tok < toks - 2, tok >= 2
    c.feature = 2 * column + parity
    c.first_segment = jnp.where(tok < 2, 1, 0)
    loads = [
        pltpu.make_async_copy(source, mine, c.w_sem.at[i])
        for i, (source, mine) in enumerate(
            (
                (r, c.my_rates),
                (bounds, c.bounds),
                (gain, c.gain),
                (gate_all.at[parity], c.wg),
                (up_all.at[parity], c.wu),
                (down_all.at[parity], c.wd),
            )
        )
    ]

    def columns(peer):
        return at(feature_of(peer, group) * width, width, width)

    def slot(t, start, size):
        return (c.k, c.v, c.q)[t].at[at((WINDOW if t < 2 else 0) + start, size, 128), :]

    owns = [
        pltpu.make_async_copy((k, v, q)[t].at[:, columns(me)], slot(t, me * rows, rows), c.own_sem.at[t])
        for t in range(3)
    ]

    def load():
        for copy in loads + owns:
            copy.start()
        loads[0].wait()
        c.rates[me] = c.my_rates[...]

    everybody = [place_of(flip(me, d, peers), tok, group) for d in range(1, peers)]
    greet(everybody, ((has_after, after), (has_before, before)), load)

    def remote(source, target, send, recv, peer):
        return pltpu.make_async_remote_copy(
            source, target, send, recv, device_id=place_of(peer, tok, group), device_id_type=MESH
        )

    def kv_copy(t, h, peer):
        return remote(
            (k, v)[t].at[pl.ds(h * part, part), columns(peer)],
            slot(t, me * rows + h * part, part),
            c.kv_send.at[t, h, peer], c.kv_recv.at[t, h, me], peer,
        )

    def q_copy(peer):
        return remote(
            q.at[:, columns(peer)], slot(2, me * rows, rows), c.q_send.at[peer], c.q_recv.at[me], peer
        )

    def rate_copy(peer):
        return remote(c.my_rates, c.rates.at[me], c.rate_send.at[peer], c.rate_recv.at[me], peer)

    def got_kv(peer, h):
        @pl.when(me != peer)
        def _():
            for t in range(2):
                target = slot(t, peer * rows + h * part, part)
                remote(target, target, c.kv_send.at[t, h, peer], c.kv_recv.at[t, h, peer], peer).wait_recv()

    def got_q(peer):
        @pl.when(me != peer)
        def _():
            target = slot(2, peer * rows, rows)
            remote(target, target, c.q_send.at[peer], c.q_recv.at[peer], peer).wait_recv()

    def got_rates(peer):
        @pl.when(me != peer)
        def _():
            target = c.rates.at[peer]
            remote(target, target, c.rate_send.at[peer], c.rate_recv.at[peer], peer).wait_recv()

    def block(peer):
        return out.at[:, columns(peer)]

    def done_rows(peer):
        return c.out.at[at(peer * rows, rows, rows), :]

    def give(peer):
        return remote(done_rows(peer), block(me), c.out_send.at[peer], c.out_recv.at[me], peer)

    def taken(peer):
        return remote(done_rows(peer), block(peer), c.out_send.at[peer], c.out_recv.at[peer], peer)

    keep = pltpu.make_async_copy(done_rows(me), block(me), c.out_own)

    def hand_out(peer):
        @pl.when(peer != me)
        def _():
            give(peer).start()

        @pl.when(peer == me)
        def _():
            keep.start()

    halos = [
        pltpu.make_async_remote_copy(
            o.at[pl.ds(c.length, WINDOW), :], o.at[pl.ds(0, WINDOW), :],
            c.halo_send.at[t], c.halo_recv.at[t], device_id=after, device_id_type=MESH,
        )
        for t, o in enumerate((c.k, c.v))
    ]

    chip = list(range(1, half))
    along = list(range(half, group))
    across = list(range(group, group + half))
    corner = list(range(group + half, peers))
    near = [d for pair in zip(along, across) for d in pair]
    everyone = chip + near + corner

    def send_kv(ds, hs=(0, 1), owner=True):
        for d in ds:
            for h in hs:
                def start():
                    for t in range(2):
                        kv_copy(t, h, flip(me, d, peers)).start()

                if h == 0 and owner:
                    pl.when(me != first_late)(start)
                else:
                    start()

    def send_q(ds):
        for d in ds:
            q_copy(flip(me, d, peers)).start()

    has_rates = (parity == 0) | (me == first_late)

    @pl.when(has_rates)
    def _():
        for d in everyone:
            rate_copy(flip(me, d, peers)).start()

    @pl.when(me == first_late)
    def _():
        send_kv(corner + near + chip, (0,), False)

    send_kv(chip + near)
    send_q(chip)

    @pl.when(parity == 1)
    def _():
        send_q(near)

    def send_corner():
        send_kv(corner)
        send_q(corner)

    pl.when((parity == 0) | (side == 0))(send_corner)

    @pl.when(parity == 0)
    def _():
        send_q(along)

    for copy in loads[1:] + owns:
        copy.wait()
    c.bound = c.bounds[tok // 2]
    transpose_down(c)
    clear_gradients(c)
    measure_start(c)

    @pl.when(tok < 2)
    def _():
        c.k[:WINDOW, :] = jnp.zeros((WINDOW, width), BF16)
        c.v[:WINDOW, :] = jnp.zeros((WINDOW, width), BF16)

    tiles = rows // (WINDOW // 2)

    def got_first_late():
        got_kv(first_late, 1)
        for p in range(group + 1, group + half):
            for h in range(2):
                got_kv(p, h)

    def got_last():
        for p in range(group + half, peers):
            for h in range(2):
                got_kv(p, h)
        for halo in halos:
            pl.when(has_after)(halo.start)

    def block_of(quarter, j):
        return quarter * half + (j + column) % half

    def attend(quarter, j):
        peer = block_of(quarter, j)
        got_q(peer)

        @pl.when((quarter == 0) & (j == 0) & has_before)
        def _():
            for halo in halos:
                halo.wait_recv()

        attention(c, peer * tiles, tiles)

    def train(i):
        p = flip_by(column, i, group)
        got_rates(p)
        for h in range(2):
            got_kv(p, h)
        train_rows(c, p, p * rows, rows)

        @pl.when(i == half - 1)
        def _():
            got_rates(first_late)
            got_kv(first_late, 0)
            train_rows(c, first_late, c.length // 2, part)

            @pl.when(parity == 1)
            def _():
                @pl.when(side == 1)
                def _():
                    for d in along:
                        q_copy(flip(me, d, peers)).wait_send()
                    send_corner()

                got_first_late()
                got_last()

        @pl.when((parity == 1) & ((i == half - 1) | ((i == half) & (side == 1))))
        def _():
            loop(half, lambda j: attend(half + 2 - i, j))

    loop(group, train)

    @pl.when((parity == 0) & (side == 0))
    def _():
        got_first_late()

    @pl.when((parity == 0) & (side == 1))
    def _():
        got_last()

    scale_gradients(c)
    for turn in range(NS_ITERS):
        sweep(c, turn)

        if turn == 1:

            @pl.when(parity == 1)
            def _():
                def step(j):
                    peer = block_of(1 - side, j)
                    attend(1 - side, j)
                    fast_old(c, peer)
                    pl.when(peer != group - 1)(functools.partial(hand_out, peer))

                loop(half, step)

    renorm(c)

    def quarter_at(s):
        early = jnp.where(side == 0, pick(s, (2, 1, 3, 0)), pick(s, (1, 3, 0, 2)))
        late = pick(s, (3 - side, side, 2 + side))
        return jnp.where(parity == 0, early, late)

    def last(step):
        s, j = step // half, step % half
        before = jnp.maximum(step - 1, 0)
        opened = block_of(quarter_at(before // half), before % half) == group - 1
        early_edge = (parity == 1) & (side == 0)

        @pl.when(((step > 0) & opened) | ((step == 0) & early_edge))
        def _():
            close_edge(c)
            hand_out(group - 1)

        quarter = quarter_at(s)

        peer = block_of(quarter, j)

        @pl.when((parity == 0) & (s == 1) & (j == 0))
        def _():
            pl.when(side == 0)(got_last)
            pl.when(side == 1)(got_first_late)
            send_q(across)

            @pl.when(side == 0)
            def _():
                for i in range(half):
                    hand_out(2 * half + i)

        @pl.when((parity == 0) | (s == 1) | ((s == 2) & (side == 0)))
        def _():
            attend(quarter, j)

        @pl.when(quarter < 2)
        def _():
            fast_old(c, peer)

        @pl.when(quarter >= 2)
        def _():
            fast_new(c, peer)

        now = (peer != group - 1) & ((parity == 1) | (side == 1) | (s > 0))
        pl.when(now)(functools.partial(hand_out, peer))

    loop(jnp.where(parity == 0, 4, 3) * half, last)
    keep.wait()
    for d in everyone:
        taken(flip(me, d, peers)).wait_recv()
    for d in everyone:
        peer = flip(me, d, peers)
        give(peer).wait_send()
        if d in along:
            pl.when((parity == 0) | (side == 0))(q_copy(peer).wait_send)
        else:
            q_copy(peer).wait_send()
        for t in range(2):
            for h in range(2):
                kv_copy(t, h, peer).wait_send()
    for halo in halos:
        pl.when(has_after)(halo.wait_send)

    @pl.when(has_rates)
    def _():
        for d in everyone:
            rate_copy(flip(me, d, peers)).wait_send()


def body(queries, keys, values, token_rates, gate_start, up_start, down_start, norm_gain, bounds):
    rows, feats = queries.shape
    group, toks = lax.axis_size("head"), lax.axis_size("tok")
    heads, width, hid_width = token_rates.shape[1], gate_start.shape[1], gate_start.shape[2]
    peers = 2 * group
    length = peers * rows
    scratch = scratch_of(length, width, hid_width, rows, peers, bounds.shape)
    return pl.pallas_call(
        functools.partial(
            kernel, tuple(scratch), sizes(length, width, hid_width, rows), group, toks
        ),
        out_shape=jax.ShapeDtypeStruct((rows, feats), BF16),
        in_specs=[pl.BlockSpec(memory_space=pltpu.HBM)] * 9,
        out_specs=pl.BlockSpec(memory_space=pl.ANY),
        scratch_shapes=list(scratch.values()),
        compiler_params=pltpu.CompilerParams(
            collective_id=0, has_side_effects=True, vmem_limit_bytes=50000000
        ),
        name="layer",
    )(
        *(
            pltpu.with_memory_space_constraint(x, pltpu.HBM)
            for x in (
                bounds, norm_gain.reshape(heads, 1, width), queries, keys, values, token_rates.T,
                gate_start, up_start, down_start,
            )
        )
    )


def solution(mesh):
    spread = P(("tok", "head"), None)
    owned = P("head", None, None)
    return jax.shard_map(
        body,
        mesh=mesh,
        in_specs=(spread,) * 4 + (owned,) * 3 + (P(), P()),
        out_specs=spread,
        check_vma=False,
    )
```

```python
import functools
import math
from types import SimpleNamespace

import jax
import jax.numpy as jnp
from jax import lax
from jax.experimental import pallas as pl
from jax.experimental.pallas import tpu as pltpu
from jax.sharding import PartitionSpec as P

AHD = 128
WINDOW = 512
NS_ITERS = 3
CHUNK = 512

linear_coef = 3.4445
cubic_coef = -4.775
quintic_coef = 2.0315
rms_epsilon = 1e-05
norm_epsilon = 1e-06
MESH = pl.DeviceIdType.MESH
F32 = jnp.float32
BF16 = jnp.bfloat16


def mm(a, b, ca=1, cb=0):
    return lax.dot_general(a, b, (((ca,), (cb,)), ((), ())), preferred_element_type=F32)


def logistic(x):
    return 0.5 * jnp.tanh(0.5 * x) + 0.5


def loop(count, fn):
    def step(i, carry):
        fn(i)
        return carry

    lax.fori_loop(0, count, step, 0)


def at(start, size, multiple):
    return pl.ds(pl.multiple_of(start, multiple), size)


def transpose_down(c):
    def step(i):
        cols = at(i * CHUNK, CHUNK, CHUNK)
        c.wdt[:, cols] = c.wd[cols, :].T

    loop(c.hid_width // CHUNK, step)


def clear_gradients(c):
    def step(i):
        c.grad[:, at(i * 64, 64, 64), :] = jnp.zeros((3, 64, c.hid_width), F32)

    loop(c.width // 64, step)


def train_rows(c, block, start, size):
    for i in range(size // 128):
        part = slice(i * 128, (i + 1) * 128)
        here = at(WINDOW + start + i * 128, 128, 128)
        rates = c.rates[block, :, part].astype(F32)
        mine = lax.broadcasted_iota(jnp.int32, rates.shape, 0) == c.feature
        rates = jnp.sum(jnp.where(mine, rates, 0.0), axis=0, keepdims=True)
        rate_col = jnp.broadcast_to(rates, (128, 128)).T[:, 0:1]
        place = start + i * 128 + lax.broadcasted_iota(jnp.int32, (128, c.width), 0)
        target = jnp.where(place < c.bound, rate_col * c.v[here, :].astype(F32), 0.0)
        c.target[part, :] = target.astype(BF16)
        c.target_t[:, part] = target.T.astype(BF16)
        c.k_t[:, part] = c.k[here, :].T
    k_rows = c.k[at(WINDOW + start, size, 128), :]
    for i in range(c.hid_width // CHUNK):
        cols = slice(i * CHUNK, (i + 1) * CHUNK)
        gate = mm(k_rows, c.wg[:, cols])
        up = mm(k_rows, c.wu[:, cols])
        sig = logistic(gate)
        act = gate * sig
        slope = up * (sig + act * (1.0 - sig))
        back = mm(c.target[:size, :], c.wdt[:, cols])
        lefts = (c.k_t, c.k_t, c.target_t)
        rights = (back * slope, back * act, act * up)
        for m, (left, right) in enumerate(zip(lefts, rights)):
            total = c.grad[m, :, cols] + mm(left[:, :size], right.astype(BF16))
            c.grad[m, :, cols] = total
            c.squares[m, :, cols] = jnp.sum((total * total).reshape(-1, 8, CHUNK), axis=0)


def scale_gradients(c):
    for m in range(3):
        frob = lax.rsqrt(jnp.sum(c.squares[m], keepdims=True) + norm_epsilon)
        c.x[0, m] = (c.grad[m] * frob).astype(BF16)


def symmetric(ref, m, size, top, corner):
    ref[m, :size, :] = top
    ref[m, size:, size:] = corner
    ref[m, size:, :size] = top[:, size:].T


def sweep(c, turn):
    old, new, h = turn % 2, (turn + 1) % 2, c.width // 2
    for m in range(3):
        x = c.x[old, m]
        top, corner = mm(x[:h], x, 1, 1), mm(x[h:], x[h:], 1, 1)
        symmetric(c.a, m, h, top.astype(BF16), corner.astype(BF16))
    for m in range(3):
        a = c.a[m]
        top = cubic_coef * a[:h].astype(F32) + quintic_coef * mm(a[:h], a)
        corner = cubic_coef * a[h:, h:].astype(F32) + quintic_coef * mm(a[h:], a[:, h:])
        symmetric(c.p, m, h, top.astype(BF16), corner.astype(BF16))
    for m in range(3):
        x = c.x[old, m]
        c.x[new, m] = (linear_coef * x.astype(F32) + mm(c.p[m], x)).astype(BF16)


def measure_start(c):
    for m, ref in ((0, c.wg), (1, c.wu)):
        for i in range(c.hid_width // CHUNK):
            cols = slice(i * CHUNK, (i + 1) * CHUNK)
            w = ref[:, cols].astype(F32)
            c.want[m, :, cols] = jnp.sqrt(jnp.sum(w * w, axis=0, keepdims=True) + norm_epsilon)

    def by_row(i):
        rows = at(i * 128, 128, 128)
        w = c.wdt[rows, :].astype(F32)
        c.want_down[rows, :] = jnp.sqrt(jnp.sum(w * w, axis=1, keepdims=True) + norm_epsilon)

    loop(c.width // 128, by_row)


def renorm(c):
    x = c.x.at[NS_ITERS % 2]
    for m, ref in ((0, c.wg), (1, c.wu)):
        for i in range(c.hid_width // CHUNK):
            cols = slice(i * CHUNK, (i + 1) * CHUNK)
            u = ref[:, cols].astype(F32) + x[m, :, cols].astype(F32)
            have = lax.rsqrt(jnp.sum(u * u, axis=0, keepdims=True) + norm_epsilon)
            x[m, :, cols] = (u * (c.want[m, :, cols] * have)).astype(BF16)
    for i in range(c.width // 128):
        rows = slice(i * 128, (i + 1) * 128)
        u = c.wdt[rows, :].astype(F32) + x[2, rows, :].astype(F32)
        have = lax.rsqrt(jnp.sum(u * u, axis=1, keepdims=True) + norm_epsilon)
        x[2, rows, :] = (u * (c.want_down[rows, :] * have)).astype(BF16)


def attention(c, first, count):
    tile = WINDOW // 2
    power = math.log2(math.e) / math.sqrt(AHD)

    def step(i):
        t = first + i
        rows = at(t * tile, tile, tile)
        span = at(t * tile, WINDOW + tile, tile)
        below = lax.broadcasted_iota(jnp.int32, (tile, tile), 1) <= lax.broadcasted_iota(
            jnp.int32, (tile, tile), 0
        )
        far_bias = jnp.where(c.first_segment * (2 - t) > 0, F32(-1e30), F32(0.0))
        mid_bias = jnp.where(c.first_segment * (1 - t) > 0, F32(-1e30), F32(0.0))
        for head in range(c.width // AHD):
            feats = slice(head * AHD, (head + 1) * AHD)
            scores = mm(c.q[rows, feats], c.k[span, feats], 1, 1)
            edge = jnp.where(below, scores[:, 2 * tile :], scores[:, :tile] + far_bias)
            mid = scores[:, tile : 2 * tile] + mid_bias
            top = jnp.max(jnp.maximum(edge, mid), axis=1, keepdims=True)
            edge = jnp.exp2((edge - top) * power)
            mid = jnp.exp2((mid - top) * power)
            total = jnp.sum(edge + mid, axis=1, keepdims=True)
            weights = jnp.concatenate(
                [
                    jnp.where(below, 0.0, edge).astype(BF16),
                    mid.astype(BF16),
                    jnp.where(below, edge, 0.0).astype(BF16),
                ],
                axis=1,
            )
            mixed = mm(weights, c.v[span, feats])
            c.out[rows, feats] = (mixed / total).astype(BF16)

    loop(count, step)


def swiglu(c, start, size, gate, up, down, down_dim):
    q_rows = c.q[at(start, size, 128), :]
    for i in range(c.hid_width // CHUNK):
        cols = slice(i * CHUNK, (i + 1) * CHUNK)
        pre_gate = mm(q_rows, gate[:, cols])
        pre_up = mm(q_rows, up[:, cols])
        c.apply_hid[:size, cols] = (pre_gate * logistic(pre_gate) * pre_up).astype(BF16)
    return mm(c.apply_hid[:size, :], down[...], 1, down_dim)


def old_rows(c, start, size):
    return swiglu(c, start, size, c.wg, c.wu, c.wd, 0)


def new_rows(c, start, size):
    new = c.x.at[NS_ITERS % 2]
    return swiglu(c, start, size, new.at[0], new.at[1], new.at[2], 1)


def finish_rows(c, start, raw):
    rows = at(start, raw.shape[0], 128)
    scale = lax.rsqrt(jnp.mean(raw * raw, axis=1, keepdims=True) + rms_epsilon)
    fast = (raw * scale * c.gain[c.feature]).astype(BF16)
    c.out[rows, :] = (c.out[rows, :].astype(F32) + fast.astype(F32)).astype(BF16)


def below_bound(c, start, shape):
    return start + lax.broadcasted_iota(jnp.int32, shape, 0) < c.bound


def fast_old(c, block):
    size = c.rows // 2
    start = block * c.rows
    c.raw[...] = old_rows(c, start, c.rows)
    finish_rows(c, start, c.raw[:size, :])

    @pl.when(start + c.rows <= c.low)
    def _():
        finish_rows(c, start + size, c.raw[size:, :])

    @pl.when(start + c.rows > c.low)
    def _():
        c.open_raw[...] = c.raw[size:, :]


def close_edge(c):
    after = new_rows(c, c.low, c.rows // 2)
    finish_rows(c, c.low, jnp.where(below_bound(c, c.low, after.shape), c.open_raw[...], after))


def fast_new(c, block):
    size = c.rows // 2
    start = block * c.rows
    c.raw[...] = new_rows(c, start, c.rows)

    @pl.when(start < c.high)
    def _():
        before = old_rows(c, start, size)
        after = c.raw[:size, :]
        c.raw[:size, :] = jnp.where(below_bound(c, start, after.shape), before, after)

    finish_rows(c, start, c.raw[...])


def scratch_of(length, width, hid_width, rows, peers, segments):
    dma = pltpu.SemaphoreType.DMA
    return {
        "q": pltpu.VMEM((length, width), BF16),
        "k": pltpu.VMEM((WINDOW + length, width), BF16),
        "v": pltpu.VMEM((WINDOW + length, width), BF16),
        "my_rates": pltpu.VMEM((peers, rows), BF16),
        "rates": pltpu.VMEM((peers, peers, rows), BF16),
        "gain": pltpu.VMEM((peers, 1, width), F32),
        "bounds": pltpu.SMEM(segments, jnp.int32),
        "out": pltpu.VMEM((length, width), BF16),
        "kv_send": dma((2, 2, peers)),
        "kv_recv": dma((2, 2, peers)),
        "q_send": dma((peers,)),
        "q_recv": dma((peers,)),
        "rate_send": dma((peers,)),
        "rate_recv": dma((peers,)),
        "own_sem": dma((3,)),
        "halo_send": dma((2,)),
        "halo_recv": dma((2,)),
        "out_send": dma((peers,)),
        "out_recv": dma((peers,)),
        "out_own": dma,
        "wg": pltpu.VMEM((width, hid_width), BF16),
        "wu": pltpu.VMEM((width, hid_width), BF16),
        "wd": pltpu.VMEM((hid_width, width), BF16),
        "wdt": pltpu.VMEM((width, hid_width), BF16),
        "target": pltpu.VMEM((rows, width), BF16),
        "target_t": pltpu.VMEM((width, rows), BF16),
        "k_t": pltpu.VMEM((width, rows), BF16),
        "grad": pltpu.VMEM((3, width, hid_width), F32),
        "squares": pltpu.VMEM((3, 8, hid_width), F32),
        "want": pltpu.VMEM((2, 1, hid_width), F32),
        "want_down": pltpu.VMEM((width, 1), F32),
        "x": pltpu.VMEM((2, 3, width, hid_width), BF16),
        "a": pltpu.VMEM((3, width, width), BF16),
        "p": pltpu.VMEM((3, width, width), BF16),
        "apply_hid": pltpu.VMEM((rows, hid_width), BF16),
        "raw": pltpu.VMEM((rows, width), F32),
        "open_raw": pltpu.VMEM((rows // 2, width), F32),
        "w_sem": dma((6,)),
    }


def sizes(length, width, hid_width, rows):
    low, high = length // 2 - length // 16, length // 2 + length // 16
    return dict(
        length=length, width=width, hid_width=hid_width, rows=rows, low=low, high=high
    )


def flip(index, distance, count):
    result, place = 0, 1
    while place < count:
        bit = (index // place) % 2
        result = result + place * (1 - bit if distance & place else bit)
        place *= 2
    return result


def flip_by(index, distance, count):
    result, place = 0, 1
    while place < count:
        bit, other = (index // place) % 2, (distance // place) % 2
        result = result + place * (bit + other - 2 * bit * other)
        place *= 2
    return result


def place_of(peer, tok, group):
    return (tok - tok % 2 + peer // group, peer % group)


def feature_of(peer, group):
    return 2 * (peer % group) + peer // group


def greet(others, neighbours, meanwhile):
    barrier = pltpu.get_barrier_semaphore()
    count = len(others)
    for other in others:
        pl.semaphore_signal(barrier, inc=1, device_id=other, device_id_type=MESH)
    for exists, other in neighbours:
        count = count + jnp.where(exists, 1, 0)

        @pl.when(exists)
        def _(other=other):
            pl.semaphore_signal(barrier, inc=1, device_id=other, device_id_type=MESH)

    meanwhile()
    pl.semaphore_wait(barrier, count)


def pick(index, values):
    result = values[-1]
    for i, value in enumerate(values[:-1]):
        result = jnp.where(index == i, value, result)
    return result


def kernel(
    names, dims, group, toks, bounds, gain, q, k, v, r, gate_all, up_all, down_all, out, *scratch
):
    c = SimpleNamespace(**dims, **dict(zip(names, scratch)))
    tok, column = lax.axis_index("tok"), lax.axis_index("head")
    parity = tok % 2
    peers, rows, width = 2 * group, c.rows, c.width
    half, part = group // 2, rows // 2
    side = column // half
    me = parity * group + column
    first_late = group
    after = ((tok + 2) % toks, column)
    before = ((tok + toks - 2) % toks, column)
    has_after, has_before = tok < toks - 2, tok >= 2
    c.feature = 2 * column + parity
    c.first_segment = jnp.where(tok < 2, 1, 0)
    loads = [
        pltpu.make_async_copy(source, mine, c.w_sem.at[i])
        for i, (source, mine) in enumerate(
            (
                (r, c.my_rates),
                (bounds, c.bounds),
                (gain, c.gain),
                (gate_all.at[parity], c.wg),
                (up_all.at[parity], c.wu),
                (down_all.at[parity], c.wd),
            )
        )
    ]

    def columns(peer):
        return at(feature_of(peer, group) * width, width, width)

    def slot(t, start, size):
        return (c.k, c.v, c.q)[t].at[at((WINDOW if t < 2 else 0) + start, size, 128), :]

    owns = [
        pltpu.make_async_copy((k, v, q)[t].at[:, columns(me)], slot(t, me * rows, rows), c.own_sem.at[t])
        for t in range(3)
    ]

    def load():
        for copy in loads + owns:
            copy.start()
        loads[0].wait()
        c.rates[me] = c.my_rates[...]

    everybody = [place_of(flip(me, d, peers), tok, group) for d in range(1, peers)]
    greet(everybody, ((has_after, after), (has_before, before)), load)

    def remote(source, target, send, recv, peer):
        return pltpu.make_async_remote_copy(
            source, target, send, recv, device_id=place_of(peer, tok, group), device_id_type=MESH
        )

    def kv_copy(t, h, peer):
        return remote(
            (k, v)[t].at[pl.ds(h * part, part), columns(peer)],
            slot(t, me * rows + h * part, part),
            c.kv_send.at[t, h, peer], c.kv_recv.at[t, h, me], peer,
        )

    def q_copy(peer):
        return remote(
            q.at[:, columns(peer)], slot(2, me * rows, rows), c.q_send.at[peer], c.q_recv.at[me], peer
        )

    def rate_copy(peer):
        return remote(c.my_rates, c.rates.at[me], c.rate_send.at[peer], c.rate_recv.at[me], peer)

    def got_kv(peer, h):
        @pl.when(me != peer)
        def _():
            for t in range(2):
                target = slot(t, peer * rows + h * part, part)
                remote(target, target, c.kv_send.at[t, h, peer], c.kv_recv.at[t, h, peer], peer).wait_recv()

    def got_q(peer):
        @pl.when(me != peer)
        def _():
            target = slot(2, peer * rows, rows)
            remote(target, target, c.q_send.at[peer], c.q_recv.at[peer], peer).wait_recv()

    def got_rates(peer):
        @pl.when(me != peer)
        def _():
            target = c.rates.at[peer]
            remote(target, target, c.rate_send.at[peer], c.rate_recv.at[peer], peer).wait_recv()

    def block(peer):
        return out.at[:, columns(peer)]

    def done_rows(peer):
        return c.out.at[at(peer * rows, rows, rows), :]

    def give(peer):
        return remote(done_rows(peer), block(me), c.out_send.at[peer], c.out_recv.at[me], peer)

    def taken(peer):
        return remote(done_rows(peer), block(peer), c.out_send.at[peer], c.out_recv.at[peer], peer)

    keep = pltpu.make_async_copy(done_rows(me), block(me), c.out_own)

    def hand_out(peer):
        @pl.when(peer != me)
        def _():
            give(peer).start()

        @pl.when(peer == me)
        def _():
            keep.start()

    halos = [
        pltpu.make_async_remote_copy(
            o.at[pl.ds(c.length, WINDOW), :], o.at[pl.ds(0, WINDOW), :],
            c.halo_send.at[t], c.halo_recv.at[t], device_id=after, device_id_type=MESH,
        )
        for t, o in enumerate((c.k, c.v))
    ]

    chip = list(range(1, half))
    along = list(range(half, group))
    across = list(range(group, group + half))
    corner = list(range(group + half, peers))
    near = [d for pair in zip(along, across) for d in pair]
    everyone = chip + near + corner

    def send_kv(ds, hs=(0, 1), owner=True):
        for d in ds:
            for h in hs:
                def start():
                    for t in range(2):
                        kv_copy(t, h, flip(me, d, peers)).start()

                if h == 0 and owner:
                    pl.when(me != first_late)(start)
                else:
                    start()

    def send_q(ds):
        for d in ds:
            q_copy(flip(me, d, peers)).start()

    has_rates = (parity == 0) | (me == first_late)

    @pl.when(has_rates)
    def _():
        for d in everyone:
            rate_copy(flip(me, d, peers)).start()

    @pl.when(me == first_late)
    def _():
        send_kv(corner + near + chip, (0,), False)

    send_kv(chip + near)
    send_q(chip)

    @pl.when(parity == 1)
    def _():
        send_q(near)

    def send_corner():
        send_kv(corner)
        send_q(corner)

    pl.when((parity == 0) | (side == 0))(send_corner)

    @pl.when(parity == 0)
    def _():
        send_q(along)

    for copy in loads[1:] + owns:
        copy.wait()
    c.bound = c.bounds[tok // 2]
    transpose_down(c)
    clear_gradients(c)
    measure_start(c)

    @pl.when(tok < 2)
    def _():
        c.k[:WINDOW, :] = jnp.zeros((WINDOW, width), BF16)
        c.v[:WINDOW, :] = jnp.zeros((WINDOW, width), BF16)

    tiles = rows // (WINDOW // 2)

    def got_first_late():
        got_kv(first_late, 1)
        for p in range(group + 1, group + half):
            for h in range(2):
                got_kv(p, h)

    def got_last():
        for p in range(group + half, peers):
            for h in range(2):
                got_kv(p, h)
        for halo in halos:
            pl.when(has_after)(halo.start)

    def block_of(quarter, j):
        return quarter * half + (j + column) % half

    def attend(quarter, j):
        peer = block_of(quarter, j)
        got_q(peer)

        @pl.when((quarter == 0) & (j == 0) & has_before)
        def _():
            for halo in halos:
                halo.wait_recv()

        attention(c, peer * tiles, tiles)

    def train(i):
        p = flip_by(column, i, group)
        got_rates(p)
        for h in range(2):
            got_kv(p, h)
        train_rows(c, p, p * rows, rows)

        @pl.when(i == half - 1)
        def _():
            got_rates(first_late)
            got_kv(first_late, 0)
            train_rows(c, first_late, c.length // 2, part)

            @pl.when(parity == 1)
            def _():
                @pl.when(side == 1)
                def _():
                    for d in along:
                        q_copy(flip(me, d, peers)).wait_send()
                    send_corner()

                got_first_late()
                got_last()

        @pl.when((parity == 1) & ((i == half - 1) | ((i == half) & (side == 1))))
        def _():
            loop(half, lambda j: attend(half + 2 - i, j))

    loop(group, train)

    @pl.when((parity == 0) & (side == 0))
    def _():
        got_first_late()

    @pl.when((parity == 0) & (side == 1))
    def _():
        got_last()

    scale_gradients(c)
    for turn in range(NS_ITERS):
        sweep(c, turn)

        if turn == 1:

            @pl.when(parity == 1)
            def _():
                def step(j):
                    peer = block_of(1 - side, j)
                    attend(1 - side, j)
                    fast_old(c, peer)
                    pl.when(peer != group - 1)(functools.partial(hand_out, peer))

                loop(half, step)

    renorm(c)

    def quarter_at(s):
        early = jnp.where(side == 0, pick(s, (2, 1, 3, 0)), pick(s, (1, 3, 0, 2)))
        late = pick(s, (3 - side, side, 2 + side))
        return jnp.where(parity == 0, early, late)

    def last(step):
        s, j = step // half, step % half
        before = jnp.maximum(step - 1, 0)
        opened = block_of(quarter_at(before // half), before % half) == group - 1
        early_edge = (parity == 1) & (side == 0)

        @pl.when(((step > 0) & opened) | ((step == 0) & early_edge))
        def _():
            close_edge(c)
            hand_out(group - 1)

        quarter = quarter_at(s)

        peer = block_of(quarter, j)

        @pl.when((parity == 0) & (s == 1) & (j == 0))
        def _():
            pl.when(side == 1)(functools.partial(send_q, across))
            pl.when(side == 0)(got_last)
            pl.when(side == 1)(got_first_late)
            pl.when(side == 0)(functools.partial(send_q, across))

            @pl.when(side == 0)
            def _():
                for i in range(half):
                    hand_out(2 * half + i)

        @pl.when((parity == 0) | (s == 1) | ((s == 2) & (side == 0)))
        def _():
            attend(quarter, j)

        @pl.when(quarter < 2)
        def _():
            fast_old(c, peer)

        @pl.when(quarter >= 2)
        def _():
            fast_new(c, peer)

        now = (peer != group - 1) & ((parity == 1) | (side == 1) | (s > 0))
        pl.when(now)(functools.partial(hand_out, peer))

    loop(jnp.where(parity == 0, 4, 3) * half, last)
    keep.wait()
    for d in everyone:
        taken(flip(me, d, peers)).wait_recv()
    for d in everyone:
        peer = flip(me, d, peers)
        give(peer).wait_send()
        if d in along:
            pl.when((parity == 0) | (side == 0))(q_copy(peer).wait_send)
        else:
            q_copy(peer).wait_send()
        for t in range(2):
            for h in range(2):
                kv_copy(t, h, peer).wait_send()
    for halo in halos:
        pl.when(has_after)(halo.wait_send)

    @pl.when(has_rates)
    def _():
        for d in everyone:
            rate_copy(flip(me, d, peers)).wait_send()


def body(queries, keys, values, token_rates, gate_start, up_start, down_start, norm_gain, bounds):
    rows, feats = queries.shape
    group, toks = lax.axis_size("head"), lax.axis_size("tok")
    heads, width, hid_width = token_rates.shape[1], gate_start.shape[1], gate_start.shape[2]
    peers = 2 * group
    length = peers * rows
    scratch = scratch_of(length, width, hid_width, rows, peers, bounds.shape)
    return pl.pallas_call(
        functools.partial(
            kernel, tuple(scratch), sizes(length, width, hid_width, rows), group, toks
        ),
        out_shape=jax.ShapeDtypeStruct((rows, feats), BF16),
        in_specs=[pl.BlockSpec(memory_space=pltpu.HBM)] * 9,
        out_specs=pl.BlockSpec(memory_space=pl.ANY),
        scratch_shapes=list(scratch.values()),
        compiler_params=pltpu.CompilerParams(
            collective_id=0, has_side_effects=True, vmem_limit_bytes=50000000
        ),
        name="layer",
    )(
        *(
            pltpu.with_memory_space_constraint(x, pltpu.HBM)
            for x in (
                bounds, norm_gain.reshape(heads, 1, width), queries, keys, values, token_rates.T,
                gate_start, up_start, down_start,
            )
        )
    )


def solution(mesh):
    spread = P(("tok", "head"), None)
    owned = P("head", None, None)
    return jax.shard_map(
        body,
        mesh=mesh,
        in_specs=(spread,) * 4 + (owned,) * 3 + (P(), P()),
        out_specs=spread,
        check_vma=False,
    )
```
